32 devices in a mesh: blocks: 2 (over y), space: 4 (over z), view: 4 (over x, core).
Axes of the slice: x: 2, y: 2, z: 4, core: 2. Of those that a mesh axis runs over, the one named last changes fastest.
Arguments:
- estimate: float32 [64, 512, 128], P('space', 'blocks'), parts along dimension 1, may hold values from 0.5 to 7.5
- observed: float32 [4, 64, 512, 128], P('view', 'space', 'blocks'), parts along dimension 2, may hold values from 0.25 to 31.5
- valid: int32 [4, 64, 512, 128], P('view', 'space', 'blocks'), parts along dimension 2, may hold values 0 or 1
- psf_spectrum: float32 [4, 2, 64, 256, 128], P('view', None, None, 'space'), may hold values from -1 to 1, as said below
Outputs:
- refined: float32 [64, 512, 128], P('space', 'blocks'), parts along dimension 1
The draws below stay inside these ranges and needn't reach their ends.
There are 2 independent parts, one for each index of `blocks`. The reference program is written for one: setup_inputs(seed, part) draws one part's arguments, and reference() takes and returns one part's arrays. A program takes and returns all parts, laid end to end along the dimension named above; an argument that names none is the same for every part. Nothing has to cross between parts.
Inputs may be any that keep to these rules, and one draw needn't show every extreme that they name: `valid`: 1 marks a voxel that the view records, 0 one that it does not. `psf_spectrum`: for each view, the discrete Fourier transform, as in the reference program, of a point-spread function that is nonnegative at every voxel and sums to one.
All inputs are finite; a program needn't handle non-finite values. No bound on the sum of `valid` on one device may be relied on, other than what follows from the above.
Results may differ from the reference program's by a relative error of at most 0.00013.
Values sent between devices are 32-bit elements; how exact they have to be, the bound alone decides.
No kernel may reach another device: no remote copies, remote signals or barrier semaphores. Data moves between devices by JAX's collectives and lax.ppermute only.
A program may use at most 128 MiB of HBM per device.

```python
import math
import jax
import jax.numpy as jnp
from jax import lax

NZ = 64
NX = 256
NY = 128
ITERS = 2
VIEWS = 4


HIGHEST = lax.Precision.HIGHEST


def signed_offset(length):
    indices = jnp.arange(length, dtype=jnp.int32)
    return ((indices + length // 2) % length - length // 2).astype(jnp.float32)


def dft_pair(length):
    indices = jnp.arange(length, dtype=jnp.int32)
    phases = indices[:, None] * indices[None, :] % length
    angles = phases.astype(jnp.float32) * (2.0 * math.pi / length)
    return (jnp.cos(angles), jnp.sin(angles))


def complex_forward(form, cosines, sines, real_part, imaginary):
    new_real = jnp.einsum(form, cosines, real_part, precision=HIGHEST) + jnp.einsum(form, sines, imaginary, precision=HIGHEST)
    new_imaginary = jnp.einsum(form, cosines, imaginary, precision=HIGHEST) - jnp.einsum(form, sines, real_part, precision=HIGHEST)
    return (new_real, new_imaginary)


def draw_estimate(key, part):
    base_key = jax.random.fold_in(key, 101)
    ground_key, spot_key, bright_key = jax.random.split(base_key, 3)
    shape = (NZ, NX, NY)
    ground = jax.random.uniform(ground_key, shape, jnp.float32, 0.5, 1.5)
    spots = jax.random.bernoulli(spot_key, 0.03, shape)
    bright = jax.random.uniform(bright_key, shape, jnp.float32, 2.0, 6.0)
    return ground + jnp.where(spots, bright, 0.0)


def draw_observed(key, part):
    base_key = jax.random.fold_in(key, 202)
    ground_key, spot_key, bright_key = jax.random.split(base_key, 3)
    shape = (VIEWS, NZ, NX, NY)
    ground = jax.random.uniform(ground_key, shape, jnp.float32, 0.5, 1.5)
    spots = jax.random.bernoulli(spot_key, 0.02, shape)
    bright = jax.random.uniform(bright_key, shape, jnp.float32, 10.0, 30.0)
    return ground + jnp.where(spots, bright, 0.0)


def draw_psf_spectrum(key, part):
    depth_off = signed_offset(NZ)[:, None, None]
    row_off = signed_offset(NX)[None, :, None]
    column_off = signed_offset(NY)[None, None, :]
    depth_cos, depth_sin = dft_pair(NZ)
    row_cos, row_sin = dft_pair(NX)
    column_cos, column_sin = dft_pair(NY)
    floor_share = 0.08
    voxel_total = NZ * NX * NY

    def one_view(view_key):
        width_key, rough_key = jax.random.split(view_key)
        picks = jax.random.uniform(width_key, (4,), jnp.float32)
        short_width = 0.8 + 0.5 * picks[0]
        side_width = 0.8 + 0.5 * picks[1]
        long_width = 8.0 + 8.0 * picks[2]
        rough = jax.random.uniform(rough_key, (NZ, NX, NY), jnp.float32, 0.5, 1.5)
        theta = 0.5 * math.pi * (picks[3] - 0.5)
        along = depth_off * jnp.cos(theta) + row_off * jnp.sin(theta)
        across = row_off * jnp.cos(theta) - depth_off * jnp.sin(theta)
        along_term = along / long_width
        across_term = across / short_width
        side_term = column_off / side_width
        quad = along_term * along_term + across_term * across_term + side_term * side_term
        kernel = jnp.exp(-0.5 * quad) * rough
        kernel = (1.0 - floor_share) * kernel / jnp.sum(kernel) + floor_share / voxel_total
        real_part = jnp.einsum('kx,zxy->zky', row_cos, kernel, precision=HIGHEST)
        imaginary = -jnp.einsum('kx,zxy->zky', row_sin, kernel, precision=HIGHEST)
        real_part, imaginary = complex_forward('ky,zxy->zxk', column_cos, column_sin, real_part, imaginary)
        real_part, imaginary = complex_forward('kz,zxy->kxy', depth_cos, depth_sin, real_part, imaginary)
        return jnp.stack((real_part, imaginary))
    return lax.map(one_view, jax.random.split(key, VIEWS))


def touch_ends(result, key, smallest, high):
    place = [jax.random.randint(jax.random.fold_in(key, axis), (), 0, length) for axis, length in enumerate(result.shape)]
    widest = result.shape.index(max(result.shape))
    beside = place[:widest] + [(place[widest] + 1) % result.shape[widest]] + place[widest + 1:]
    return result.at[tuple(place)].set(smallest).at[tuple(beside)].set(high)


def setup_inputs(seed: int = 0, part: int = 0) -> dict:
    streams_of = jax.random.split(jax.random.key(seed), 5)
    part_keys = jax.random.split(jax.random.fold_in(streams_of[4], part), 5)
    return {
        "estimate": draw_estimate(jax.random.fold_in(jax.random.fold_in(streams_of[4], part), 71), part),
        "observed": draw_observed(jax.random.fold_in(jax.random.fold_in(streams_of[4], part), 71), part),
        "valid": touch_ends((jax.random.randint(part_keys[2], (VIEWS, NZ, NX, NY), 0, 4) < 3).astype(jnp.int32), jax.random.fold_in(part_keys[2], 1), 0, 1),
        "psf_spectrum": draw_psf_spectrum(jax.random.fold_in(streams_of[4], 71), part),
    }


def reference(estimate, observed, valid, psf_spectrum):
    view_count = observed.shape[0]
    for iteration in range(ITERS):
        spectrum = jnp.fft.fftn(estimate)

        def one_view(accumulated, items):
            observed_view, valid_view, kernel = items
            transfer = lax.complex(kernel[0], kernel[1])
            blurred = jnp.real(jnp.fft.ifftn(spectrum * transfer))
            valid_mask = valid_view.astype(jnp.float32)
            ratios = valid_mask * observed_view / blurred + (1.0 - valid_mask)
            correction = jnp.real(jnp.fft.ifftn(jnp.fft.fftn(ratios) * jnp.conj(transfer)))
            return accumulated + correction, None

        combined, unused = lax.scan(one_view, jnp.zeros_like(estimate), (observed, valid, psf_spectrum))
        estimate = estimate * combined / view_count
    return estimate
```

```python
import functools

import jax
import jax.numpy as jnp
import ml_dtypes
import numpy as np
from jax import lax
from jax.experimental import pallas as pl
from jax.experimental.pallas import tpu as pltpu
from jax.sharding import PartitionSpec as P

ITERS = 2
INTERPRET = False


def split_np(matrix):
    high = matrix.astype(ml_dtypes.bfloat16)
    low = (matrix - high.astype(np.float64)).astype(ml_dtypes.bfloat16)
    return high, low


def angles_np(length):
    index = np.arange(length)
    return (np.outer(index, index) % length) * (2.0 * np.pi / length)


def column_tables(length, scale):
    half = length // 2
    angles = angles_np(length)
    cosines, sines = np.cos(angles), np.sin(angles)
    alternating = np.where(np.arange(length) % 2 == 0, 1.0, -1.0)
    forward = np.zeros((length, length))
    forward[:, :half] = cosines[:, :half]
    forward[:, half:] = -sines[:, :half]
    forward[:, half] = alternating
    inverse = np.zeros((length, length))
    inverse[:half] = 2.0 * cosines[:half]
    inverse[half:] = -2.0 * sines[:half]
    inverse[0] = 1.0
    inverse[half] = alternating
    inverse *= scale
    tables = []
    for matrix in (forward, inverse):
        high, low = split_np(matrix)
        both = np.concatenate([high, low], axis=1)
        tables.append(np.concatenate([both, both], axis=0))
    return tables


def row_tables(length, lanes):
    middle, half = length // 2, lanes // 2
    angles = angles_np(length)
    cosines, sines = np.cos(angles), np.sin(angles)
    sines[0] = -cosines[middle]
    sines[middle] = -cosines[0]
    high, low = split_np(np.concatenate([cosines, sines], axis=0))
    forward = np.concatenate([high, low], axis=0)
    high, low = split_np(np.concatenate([cosines.T, sines.T], axis=1))
    inverse = np.concatenate([high, low], axis=0)
    row = np.arange(length)[:, None]
    lane = np.arange(lanes)[None, :]
    plain = (lane % half) != 0
    lower = row < middle
    inner = (row % middle) != 0
    first, second = lane == 0, lane == half
    sign = np.where(lane < half, 1.0, -1.0)
    weight = np.where(inner, 2.0, 1.0)
    one = np.ones((length, lanes))
    forward_masks = np.stack(
        [
            one * (plain | (first & lower)),
            one * (first & ~lower),
            -one * (second & ~lower),
            sign * (plain & inner) - one * (second & lower),
        ]
    )
    inverse_masks = np.stack(
        [
            one * plain + weight * (first & lower),
            weight * (second & ~lower),
            -weight * (second & ~lower),
            -sign * (plain & inner) - weight * (first & lower),
        ]
    )
    return forward, inverse, forward_masks.astype(np.float32), inverse_masks.astype(np.float32)


def depth_forward(order):
    angles = angles_np(len(order))[:, order]
    high, low = split_np(np.concatenate([np.cos(angles), np.sin(angles)], axis=0))
    both = np.concatenate([high, low], axis=0)
    return np.concatenate([both, both], axis=1)


def depth_inverse(order):
    angles = angles_np(len(order))[order, :]
    high, low = split_np(np.concatenate([np.cos(angles), np.sin(angles)], axis=0))
    both = np.concatenate([high, low], axis=0)
    return np.concatenate([both, both], axis=1)


def split(value):
    high = value.astype(jnp.bfloat16)
    low = (value - high.astype(jnp.float32)).astype(jnp.bfloat16)
    return high, low


def dot(left, right):
    return lax.dot_general(
        left, right, (((1,), (0,)), ((), ())), preferred_element_type=jnp.float32
    )


def fold_lanes(value):
    lanes = value.shape[1] // 2
    return value[:, :lanes] + value[:, lanes:]


def fold_rows(value):
    rows = value.shape[0] // 2
    return value[:rows] + value[rows:]


def plane_forward(plane, columns, rows, masks):
    step = fold_lanes(dot(jnp.concatenate(split(plane), axis=1), columns[...]))
    both = fold_lanes(fold_rows(dot(rows[...], jnp.concatenate(split(step), axis=1))))
    count, half = both.shape[0] // 2, both.shape[1] // 2
    cos_part, sin_part = both[:count], both[count:]
    return (
        cos_part * masks[0]
        + pltpu.roll(cos_part, half, 1) * masks[1]
        + sin_part * masks[2]
        + pltpu.roll(sin_part, half, 1) * masks[3]
    )


def plane_inverse(spectrum, columns, rows, masks):
    rolled = pltpu.roll(spectrum, spectrum.shape[1] // 2, 1)
    both = jnp.concatenate(
        [spectrum * masks[0] + rolled * masks[1], spectrum * masks[2] + rolled * masks[3]], axis=0
    )
    step = fold_lanes(fold_rows(dot(rows[...], jnp.concatenate(split(both), axis=1))))
    return fold_lanes(dot(jnp.concatenate(split(step), axis=1), columns[...]))


def whole_spec(array):
    rank = array.ndim
    return pl.BlockSpec(array.shape, lambda *_: (0,) * rank)


def read_plane(ref, index):
    return ref[:, index].reshape(-1, ref.shape[-1])


def write_plane(ref, index, value):
    ref[:, index] = value.reshape(ref.shape[0], ref.shape[2], ref.shape[3])


def step_planes(planes):
    return 2 if planes % 2 == 0 else 1


def lateral_forward(volume, tables, parts):
    planes, rows, lanes = volume.shape
    step = step_planes(planes)

    def body(volume_ref, columns, row_table, masks, out_ref):
        for index in range(step):
            write_plane(out_ref, index, plane_forward(volume_ref[index], columns, row_table, masks))

    constants = (tables["columns_f"], tables["rows_f"], tables["masks_f"])
    return pl.pallas_call(
        body,
        grid=(planes // step,),
        out_shape=jax.ShapeDtypeStruct((parts, planes, rows // parts, lanes), jnp.float32),
        in_specs=[pl.BlockSpec((step, rows, lanes), lambda i: (i, 0, 0))]
        + [whole_spec(c) for c in constants],
        out_specs=pl.BlockSpec((parts, step, rows // parts, lanes), lambda i: (0, i, 0, 0)),
        interpret=INTERPRET,
        name="lateral_forward",
    )(volume, *constants)


def ratio_step(spectrum, observed, valid, tables):
    parts, planes, part_rows, lanes = spectrum.shape
    rows = parts * part_rows
    step = step_planes(planes)

    def body(
        spectrum_ref, observed_ref, valid_ref, columns_i, rows_i, masks_i, columns_f, rows_f, masks_f, out_ref
    ):
        for index in range(step):
            blurred = plane_inverse(read_plane(spectrum_ref, index), columns_i, rows_i, masks_i)
            mask = valid_ref[index].astype(jnp.float32)
            ratio = mask * observed_ref[index] / blurred + (1.0 - mask)
            write_plane(out_ref, index, plane_forward(ratio, columns_f, rows_f, masks_f))

    constants = tuple(
        tables[name] for name in ("columns_i", "rows_i", "masks_i", "columns_f", "rows_f", "masks_f")
    )
    block = pl.BlockSpec((parts, step, part_rows, lanes), lambda i: (0, i, 0, 0))
    plane = pl.BlockSpec((step, rows, lanes), lambda i: (i, 0, 0))
    return pl.pallas_call(
        body,
        grid=(planes // step,),
        out_shape=jax.ShapeDtypeStruct(spectrum.shape, jnp.float32),
        in_specs=[block, plane, plane] + [whole_spec(c) for c in constants],
        out_specs=block,
        interpret=INTERPRET,
        name="ratio_step",
    )(spectrum, observed, valid, *constants)


def update_step(spectrum, estimate, view_count, tables, last):
    parts, planes, part_rows, lanes = spectrum.shape
    rows = parts * part_rows
    step = step_planes(planes)

    def body(spectrum_ref, estimate_ref, columns_i, rows_i, masks_i, columns_f, rows_f, masks_f, *outs):
        for index in range(step):
            combined = plane_inverse(read_plane(spectrum_ref, index), columns_i, rows_i, masks_i)
            updated = estimate_ref[index] * combined / view_count
            outs[0][index] = updated
            if not last:
                write_plane(outs[1], index, plane_forward(updated, columns_f, rows_f, masks_f))

    constants = tuple(
        tables[name] for name in ("columns_i", "rows_i", "masks_i", "columns_f", "rows_f", "masks_f")
    )
    block = pl.BlockSpec((parts, step, part_rows, lanes), lambda i: (0, i, 0, 0))
    plane = pl.BlockSpec((step, rows, lanes), lambda i: (i, 0, 0))
    shapes = [
        jax.ShapeDtypeStruct(estimate.shape, jnp.float32),
        jax.ShapeDtypeStruct(spectrum.shape, jnp.float32),
    ]
    count = 1 if last else 2
    return pl.pallas_call(
        body,
        grid=(planes // step,),
        out_shape=shapes[:count],
        in_specs=[block, plane] + [whole_spec(c) for c in constants],
        out_specs=[plane, block][:count],
        interpret=INTERPRET,
        name="update_step",
    )(spectrum, estimate, *constants)


def depth_step(pieces, transfer, forward, inverse, out_planes, adjoint):
    parts, _, rows, lanes = pieces[0].shape
    half = lanes // 2
    block_rows = 8
    depth = sum(p.shape[1] for p in pieces) * parts
    main, cross = transfer
    in_count = len(pieces)

    def body(*refs):
        ins = refs[:in_count]
        main_ref, cross_ref, forward_ref, inverse_ref = refs[in_count : in_count + 4]
        outs = refs[in_count + 4 :]
        lane = lax.broadcasted_iota(jnp.int32, (depth, lanes), 1)
        sign = jnp.where(lane < half, 1.0, -1.0)
        side = -1.0 if adjoint else 1.0
        for pair in range(block_rows // 2):
            columns = []
            for k in (2 * pair, 2 * pair + 1):
                columns.append(
                    jnp.concatenate(
                        [
                            ref.reshape(parts * ref.shape[1] * block_rows, lanes)[
                                pl.ds(k, parts * ref.shape[1], stride=block_rows), :
                            ]
                            for ref in ins
                        ],
                        axis=0,
                    )
                )
            both = jnp.concatenate(columns, axis=1)
            grown = fold_rows(dot(forward_ref[...], jnp.concatenate(split(both), axis=0)))
            results = []
            for index in range(2):
                k = 2 * pair + index
                lanes_of = slice(index * lanes, (index + 1) * lanes)
                cos_part, sin_part = grown[:depth, lanes_of], grown[depth:, lanes_of]
                sin_roll = pltpu.roll(sin_part, half, 1)
                spectrum = cos_part + sign * sin_roll
                result = (
                    spectrum * main_ref[0, k]
                    + pltpu.roll(spectrum, half, 1) * main_ref[1, k] * side
                )
                if k == 0:
                    mirrored = sign * cos_part - sin_roll
                    extra = (
                        mirrored * cross_ref[0]
                        + pltpu.roll(mirrored, half, 1) * cross_ref[1] * side
                    )
                    result = result + jnp.where(pl.program_id(0) == 0, extra, 0.0)
                results.append(result)
            both = jnp.concatenate(results, axis=1)
            grown = fold_rows(dot(inverse_ref[...], jnp.concatenate(split(both), axis=0)))
            for index in range(2):
                k = 2 * pair + index
                lanes_of = slice(index * lanes, (index + 1) * lanes)
                cos_part, sin_part = grown[:depth, lanes_of], grown[depth:, lanes_of]
                volume = cos_part - sign * pltpu.roll(sin_part, half, 1)
                start = 0
                for ref in outs:
                    count = parts * ref.shape[1]
                    ref.reshape(count * block_rows, lanes)[
                        pl.ds(k, count, stride=block_rows), :
                    ] = volume[start : start + count]
                    start += count

    def piece_spec(planes):
        return pl.BlockSpec((parts, planes, block_rows, lanes), lambda i: (0, 0, i, 0))

    return pl.pallas_call(
        body,
        grid=(rows // block_rows,),
        out_shape=[jax.ShapeDtypeStruct((parts, n, rows, lanes), jnp.float32) for n in out_planes],
        in_specs=[piece_spec(p.shape[1]) for p in pieces]
        + [
            pl.BlockSpec((2, block_rows, depth, lanes), lambda i: (0, i, 0, 0)),
            whole_spec(cross),
            whole_spec(forward),
            whole_spec(inverse),
        ],
        out_specs=[piece_spec(n) for n in out_planes],
        interpret=INTERPRET,
        name="depth_step",
    )(*pieces, main, cross, forward, inverse)


def transfer_tables(psf, space_count):
    half = psf.shape[-1] // 2
    device = lax.axis_index("space")
    upper = device >= space_count // 2
    special = (device % (space_count // 2)) == 0
    pairs = [(0, space_count // 2), (space_count // 2, 0)]
    own = jnp.where(upper, psf[:, :, 0, half], psf[:, :, 0, 0])
    given = jnp.where(upper, psf[:, :, 0, 0], psf[:, :, 0, half])
    other = lax.ppermute(given, "space", pairs)
    mean = jnp.where(special, 0.5 * (own + other), own)
    cross = jnp.where(special, 0.5 * (own - other), jnp.zeros_like(own))
    column = jnp.where(upper, psf[..., half], psf[..., 0])
    first_row = lax.broadcasted_iota(jnp.int32, column.shape, 2) == 0
    column = jnp.where(first_row, mean[:, :, None], column)
    first_lane = lax.broadcasted_iota(jnp.int32, psf.shape[:3] + (half,), 3) == 0
    packed = jnp.where(first_lane, column[..., None], psf[..., :half])
    packed = packed.transpose(0, 2, 1, 3)
    main = jnp.stack(
        [
            jnp.concatenate([packed[0], packed[0]], axis=-1),
            jnp.concatenate([-packed[1], packed[1]], axis=-1),
        ]
    )
    lane = lax.broadcasted_iota(jnp.int32, (psf.shape[1], 2 * half), 1)
    cross = jnp.stack(
        [
            jnp.where(lane % half == 0, cross[0][:, None], 0.0),
            jnp.where(lane == 0, -cross[1][:, None], jnp.where(lane == half, cross[1][:, None], 0.0)),
        ]
    )
    return main, cross


def exchange(array):
    return lax.all_to_all(array, "space", split_axis=0, concat_axis=0, tiled=True)


def partner(array, count, stride):
    return lax.ppermute(array, "view", [(i, i ^ stride) for i in range(count)])


def shards(estimate, observed, valid, psf_spectrum):
    space_count = lax.axis_size("space")
    views = lax.axis_size("view")
    planes, row_total, lanes = estimate.shape
    depth_total = planes * space_count
    view_count = views * observed.shape[0]
    columns_f, columns_i = column_tables(lanes, 1.0 / (depth_total * row_total * lanes))
    rows_f, rows_i, masks_f, masks_i = row_tables(row_total, lanes)
    tables = {
        "columns_f": jnp.asarray(columns_f),
        "columns_i": jnp.asarray(columns_i),
        "rows_f": jnp.asarray(rows_f),
        "rows_i": jnp.asarray(rows_i),
        "masks_f": jnp.asarray(masks_f),
        "masks_i": jnp.asarray(masks_i),
    }
    observed, valid = observed[0], valid[0]
    transfer = transfer_tables(psf_spectrum[0], space_count)

    shared = planes % views == 0 and views & (views - 1) == 0
    blocks = views if shared else 1
    share = planes // blocks
    strides = []
    while 1 << len(strides) < blocks:
        strides.append(1 << len(strides))
    flips = [0]
    for stride in reversed(strides):
        flips = flips + [f ^ stride for f in flips]
    slabs = np.arange(space_count)[:, None] * planes

    def order_of(starts, count):
        return np.concatenate([(slabs + start + np.arange(count)[None, :]).reshape(-1) for start in starts])

    if shared:
        me = lax.axis_index("view")
        view_orders = [order_of([(v ^ f) * share for f in flips], share) for v in range(views)]
        view_forward = jnp.asarray(np.stack([depth_forward(o) for o in view_orders]))[me]
        view_inverse = jnp.asarray(np.stack([depth_inverse(o) for o in view_orders]))[me]
        own = lax.dynamic_slice_in_dim(estimate, me * share, share, 0)
    else:
        view_forward = jnp.asarray(depth_forward(order_of([0], planes)))
        view_inverse = jnp.asarray(depth_inverse(order_of([0], planes)))
        own = estimate
    slab_forward = jnp.asarray(depth_forward(order_of([0], planes)))
    slab_inverse = jnp.asarray(depth_inverse(order_of([0], planes)))

    spectrum = lateral_forward(own, tables, space_count)
    for iteration in range(ITERS):
        last = iteration == ITERS - 1
        pieces = [exchange(spectrum)]
        for stride in reversed(strides):
            pieces = pieces + [partner(p, views, stride) for p in pieces]
        (blurred,) = depth_step(pieces, transfer, view_forward, slab_inverse, [planes], False)
        ratios = ratio_step(exchange(blurred), observed, valid, tables)
        parts = depth_step(
            [exchange(ratios)], transfer, slab_forward, view_inverse, [share] * blocks, True
        )
        if shared:
            for stride in strides:
                middle = len(parts) // 2
                moved = [partner(p, views, stride) for p in parts[middle:]]
                parts = [kept + new for kept, new in zip(parts[:middle], moved)]
            total = parts[0]
        else:
            total = lax.psum(parts[0], "view")
        results = update_step(exchange(total), own, float(view_count), tables, last)
        own = results[0]
        if not last:
            spectrum = results[1]
    if shared:
        own = lax.all_gather(own, "view", axis=0, tiled=True)
    return own


def solution(mesh):
    return jax.shard_map(
        shards,
        mesh=mesh,
        in_specs=(
            P("space", "blocks", None),
            P("view", "space", "blocks", None),
            P("view", "space", "blocks", None),
            P("view", None, None, "space", None),
        ),
        out_specs=P("space", "blocks", None),
        check_vma=False,
    )
```

```python
import functools

import jax
import jax.numpy as jnp
import ml_dtypes
import numpy as np
from jax import lax
from jax.experimental import pallas as pl
from jax.experimental.pallas import tpu as pltpu
from jax.sharding import PartitionSpec as P

ITERS = 2
INTERPRET = False


def split_np(matrix):
    high = matrix.astype(ml_dtypes.bfloat16)
    low = (matrix - high.astype(np.float64)).astype(ml_dtypes.bfloat16)
    return high, low


def angles_np(length):
    index = np.arange(length)
    return (np.outer(index, index) % length) * (2.0 * np.pi / length)


def column_tables(length, scale):
    half = length // 2
    angles = angles_np(length)
    cosines, sines = np.cos(angles), np.sin(angles)
    alternating = np.where(np.arange(length) % 2 == 0, 1.0, -1.0)
    forward = np.zeros((length, length))
    forward[:, :half] = cosines[:, :half]
    forward[:, half:] = -sines[:, :half]
    forward[:, half] = alternating
    inverse = np.zeros((length, length))
    inverse[:half] = 2.0 * cosines[:half]
    inverse[half:] = -2.0 * sines[:half]
    inverse[0] = 1.0
    inverse[half] = alternating
    inverse *= scale
    tables = []
    for matrix in (forward, inverse):
        high, low = split_np(matrix)
        both = np.concatenate([high, low], axis=1)
        tables.append(np.concatenate([both, both], axis=0))
    return tables


def row_tables(length, lanes):
    middle, half = length // 2, lanes // 2
    angles = angles_np(length)
    cosines, sines = np.cos(angles), np.sin(angles)
    sines[0] = -cosines[middle]
    sines[middle] = -cosines[0]
    high, low = split_np(np.concatenate([cosines, sines], axis=0))
    forward = np.concatenate([high, low], axis=0)
    high, low = split_np(np.concatenate([cosines.T, sines.T], axis=1))
    inverse = np.concatenate([high, low], axis=0)
    row = np.arange(length)[:, None]
    lane = np.arange(lanes)[None, :]
    plain = (lane % half) != 0
    lower = row < middle
    inner = (row % middle) != 0
    first, second = lane == 0, lane == half
    sign = np.where(lane < half, 1.0, -1.0)
    weight = np.where(inner, 2.0, 1.0)
    one = np.ones((length, lanes))
    forward_masks = np.stack(
        [
            one * (plain | (first & lower)),
            one * (first & ~lower),
            -one * (second & ~lower),
            sign * (plain & inner) - one * (second & lower),
        ]
    )
    inverse_masks = np.stack(
        [
            one * plain + weight * (first & lower),
            weight * (second & ~lower),
            -weight * (second & ~lower),
            -sign * (plain & inner) - weight * (first & lower),
        ]
    )
    return forward, inverse, forward_masks.astype(np.float32), inverse_masks.astype(np.float32)


def split(value):
    high = value.astype(jnp.bfloat16)
    low = (value - high.astype(jnp.float32)).astype(jnp.bfloat16)
    return high, low


def dot(left, right):
    return lax.dot_general(
        left, right, (((1,), (0,)), ((), ())), preferred_element_type=jnp.float32
    )


def fold_lanes(value):
    lanes = value.shape[1] // 2
    return value[:, :lanes] + value[:, lanes:]


def fold_rows(value):
    rows = value.shape[0] // 2
    return value[:rows] + value[rows:]


def plane_forward(plane, columns, rows, masks):
    step = fold_lanes(dot(jnp.concatenate(split(plane), axis=1), columns[...]))
    both = fold_lanes(fold_rows(dot(rows[...], jnp.concatenate(split(step), axis=1))))
    count, half = both.shape[0] // 2, both.shape[1] // 2
    cos_part, sin_part = both[:count], both[count:]
    return (
        cos_part * masks[0]
        + pltpu.roll(cos_part, half, 1) * masks[1]
        + sin_part * masks[2]
        + pltpu.roll(sin_part, half, 1) * masks[3]
    )


def plane_inverse(spectrum, columns, rows, masks):
    rolled = pltpu.roll(spectrum, spectrum.shape[1] // 2, 1)
    both = jnp.concatenate(
        [spectrum * masks[0] + rolled * masks[1], spectrum * masks[2] + rolled * masks[3]], axis=0
    )
    step = fold_lanes(fold_rows(dot(rows[...], jnp.concatenate(split(both), axis=1))))
    return fold_lanes(dot(jnp.concatenate(split(step), axis=1), columns[...]))


def depth_table(order, depth, inverse):
    frequency = jnp.arange(depth, dtype=jnp.int32)
    if inverse:
        phases = order[:, None] * frequency[None, :] % depth
    else:
        phases = frequency[:, None] * order[None, :] % depth
    angles = phases.astype(jnp.float32) * (2.0 * np.pi / depth)
    matrix = jnp.concatenate([jnp.cos(angles), jnp.sin(angles)], axis=0)
    high = lax.reduce_precision(matrix, 8, 7)
    both = jnp.concatenate([high, matrix - high], axis=0)
    return jnp.concatenate([both, both], axis=1).astype(jnp.bfloat16)


def whole_spec(array):
    rank = array.ndim
    return pl.BlockSpec(array.shape, lambda *_: (0,) * rank)


def start_of(device_ref, k, count):
    return pl.multiple_of(jnp.bitwise_xor(device_ref[0], k) * count, count)


def gather_rows(device_ref, refs, index, scratch):
    count = refs[0].shape[1]
    for k, ref in enumerate(refs):
        scratch[index, pl.ds(start_of(device_ref, k, count), count), :] = ref[index]
    return scratch[index]


def scatter_rows(device_ref, refs, index, scratch, value):
    count = refs[0].shape[1]
    scratch[index] = value
    for k, ref in enumerate(refs):
        ref[index] = scratch[index, pl.ds(start_of(device_ref, k, count), count), :]


def lateral_call(body, name, planes, rows, lanes, parts, device, operands, offsets, pieces, constants, out_planes, out_pieces):
    step = 2 if planes % 2 == 0 else 1
    count = rows // parts
    piece = pl.BlockSpec((step, count, lanes), lambda i, *_: (i, 0, 0))
    plane = pl.BlockSpec((step, rows, lanes), lambda i, *_: (i, 0, 0))

    def plane_at(offset):
        return pl.BlockSpec((step, rows, lanes), lambda i, *_: (i + offset // step, 0, 0))

    def kernel(device_ref, *refs):
        spans = np.cumsum([0, len(operands), len(pieces), len(constants), out_planes, out_pieces, 2])
        groups = [refs[a:b] for a, b in zip(spans[:-1], spans[1:])]
        for index in range(step):
            body(device_ref, index, *groups)

    return pl.pallas_call(
        kernel,
        grid_spec=pltpu.PrefetchScalarGridSpec(
            num_scalar_prefetch=1,
            grid=(planes // step,),
            in_specs=[plane_at(o) for o in offsets]
            + [piece] * len(pieces)
            + [whole_spec(c) for c in constants],
            out_specs=[plane] * out_planes + [piece] * out_pieces,
            scratch_shapes=[pltpu.VMEM((step, rows, lanes), jnp.float32)] * 2,
        ),
        out_shape=[jax.ShapeDtypeStruct((planes, rows, lanes), jnp.float32)] * out_planes
        + [jax.ShapeDtypeStruct((planes, count, lanes), jnp.float32)] * out_pieces,
        interpret=INTERPRET,
        name=name,
    )(device, *operands, *pieces, *constants)


def lateral_forward(volume, device, tables, parts):
    planes, rows, lanes = volume.shape

    def body(device_ref, index, ins, _, constants, __, outs, scratch):
        value = plane_forward(ins[0][index], *constants)
        scatter_rows(device_ref, outs, index, scratch[0], value)

    return lateral_call(
        body, "lateral_forward", planes, rows, lanes, parts, device,
        [volume], [0], [], tables["forward"], 0, parts,
    )


def ratio_step(pieces, observed, valid, offset, device, tables):
    planes, part_rows, lanes = pieces[0].shape
    parts = len(pieces)

    def body(device_ref, index, ins, spectrum, constants, _, outs, scratch):
        value = gather_rows(device_ref, spectrum, index, scratch[0])
        blurred = plane_inverse(value, *constants[:3])
        mask = ins[1][index].astype(jnp.float32)
        ratio = mask * ins[0][index] / blurred + (1.0 - mask)
        value = plane_forward(ratio, *constants[3:])
        scatter_rows(device_ref, outs, index, scratch[1], value)

    return lateral_call(
        body, "ratio_step", planes, parts * part_rows, lanes, parts, device,
        [observed, valid], [offset, offset], pieces, tables["inverse"] + tables["forward"], 0, parts,
    )


def update_step(pieces, estimate, view_count, device, tables, last):
    planes, part_rows, lanes = pieces[0].shape
    parts = len(pieces)

    def body(device_ref, index, ins, spectrum, constants, planes_out, outs, scratch):
        value = gather_rows(device_ref, spectrum, index, scratch[0])
        combined = plane_inverse(value, *constants[:3])
        updated = ins[0][index] * combined / view_count
        planes_out[0][index] = updated
        if not last:
            value = plane_forward(updated, *constants[3:])
            scatter_rows(device_ref, outs, index, scratch[1], value)

    constants = tables["inverse"] + (() if last else tables["forward"])
    results = lateral_call(
        body, "update_step", planes, parts * part_rows, lanes, parts, device,
        [estimate], [0], pieces, constants, 1, 0 if last else parts,
    )
    return results[0], results[1:]


BLOCK_ROWS = 8


def rows_of(ref, k):
    planes, count, lanes = ref.shape
    return ref.reshape(planes * count, lanes).at[pl.ds(k, planes, stride=count), :]


def depth_step(pieces, added, transfer, forward, inverse, out_planes, keep, adjoint, depth):
    main, cross = transfer
    _, rows, _, lanes = main.shape
    half = lanes // 2
    block = BLOCK_ROWS
    stored = pl.BlockSpec((block, depth, lanes), lambda i: (i, 0, 0))
    operands, specs = [], []

    def piece_spec(planes):
        return pl.BlockSpec((planes, block, lanes), lambda i: (0, i, 0))

    for piece in pieces:
        operands.append(piece)
        specs.append(piece_spec(piece.shape[0]))
    if pieces:
        operands += [main, cross, forward]
        specs += [
            pl.BlockSpec((2, block, depth, lanes), lambda i: (0, i, 0, 0)),
            whole_spec(cross),
            whole_spec(forward),
        ]
    if added is not None:
        operands.append(added)
        specs.append(stored)
    if out_planes:
        operands.append(inverse)
        specs.append(whole_spec(inverse))
    out_shape = [jax.ShapeDtypeStruct((n, rows, lanes), jnp.float32) for n in out_planes]
    out_specs = [piece_spec(n) for n in out_planes]
    if keep:
        out_shape.append(jax.ShapeDtypeStruct((rows, depth, lanes), jnp.float32))
        out_specs.append(stored)
    side = -1.0 if adjoint else 1.0

    def body(*refs):
        refs = list(refs)
        ins = [refs.pop(0) for _ in pieces]
        if pieces:
            main_ref, cross_ref, forward_ref = refs.pop(0), refs.pop(0), refs.pop(0)
        added_ref = refs.pop(0) if added is not None else None
        inverse_ref = refs.pop(0) if out_planes else None
        outs = [refs.pop(0) for _ in out_planes]
        keep_ref = refs.pop(0) if keep else None

        def sign(count):
            lane = lax.broadcasted_iota(jnp.int32, (count, lanes), 1)
            return jnp.where(lane < half, 1.0, -1.0)

        for pair in range(block // 2):
            ks = (2 * pair, 2 * pair + 1)
            results = []
            if pieces:
                columns = [jnp.concatenate([rows_of(ref, k)[...] for ref in ins], axis=0) for k in ks]
                both = jnp.concatenate(columns, axis=1)
                grown = fold_rows(dot(forward_ref[...], jnp.concatenate(split(both), axis=0)))
                for index, k in enumerate(ks):
                    lanes_of = slice(index * lanes, (index + 1) * lanes)
                    cos_part, sin_part = grown[:depth, lanes_of], grown[depth:, lanes_of]
                    sin_roll = pltpu.roll(sin_part, half, 1)
                    spectrum = cos_part + sign(depth) * sin_roll
                    result = (
                        spectrum * main_ref[0, k]
                        + pltpu.roll(spectrum, half, 1) * main_ref[1, k] * side
                    )
                    if k == 0:
                        change = sign(depth) * cos_part - sin_roll - spectrum
                        extra = (
                            change * cross_ref[0]
                            + pltpu.roll(change, half, 1) * cross_ref[1] * side
                        )
                        result = result + jnp.where(pl.program_id(0) == 0, extra, 0.0)
                    if added is not None:
                        result = result + added_ref[k]
                    results.append(result)
            else:
                results = [added_ref[k] for k in ks]
            if keep:
                for k, result in zip(ks, results):
                    keep_ref[k] = result
            if not out_planes:
                continue
            total = sum(out_planes)
            both = jnp.concatenate(results, axis=1)
            grown = fold_rows(dot(inverse_ref[...], jnp.concatenate(split(both), axis=0)))
            for index, k in enumerate(ks):
                lanes_of = slice(index * lanes, (index + 1) * lanes)
                cos_part, sin_part = grown[:total, lanes_of], grown[total:, lanes_of]
                volume = cos_part - sign(total) * pltpu.roll(sin_part, half, 1)
                start = 0
                for ref in outs:
                    rows_of(ref, k)[...] = volume[start : start + ref.shape[0]]
                    start += ref.shape[0]

    results = pl.pallas_call(
        body,
        grid=(rows // block,),
        out_shape=out_shape,
        in_specs=specs,
        out_specs=out_specs,
        interpret=INTERPRET,
        name="depth_step",
    )(*operands)
    outs = results[: len(out_planes)]
    return outs, (results[-1] if keep else None)


def transfer_tables(psf, after, space_count):
    _, depth, rows, lanes = psf.shape
    half = lanes // 2
    device = lax.axis_index("space")
    upper = device >= space_count // 2
    special = (device % (space_count // 2)) == 0
    block = BLOCK_ROWS

    def body(upper_ref, psf_ref, _, main_ref, first_ref):
        lane = lax.broadcasted_iota(jnp.int32, (depth, lanes), 1)
        for k in range(block):
            for part in range(2):
                value = rows_of(psf_ref.at[part], k)[...]
                if k == 0:
                    first_ref[part] = value
                rolled = pltpu.roll(value, half, 1)
                doubled = jnp.where(lane < half, value, rolled)
                other = jnp.where(lane < half, rolled, value)
                packed = jnp.where((lane % half == 0) & (upper_ref[0] > 0), other, doubled)
                if part == 1:
                    packed = jnp.where(lane < half, -packed, packed)
                main_ref[part, k] = packed

    main, first = pl.pallas_call(
        body,
        grid_spec=pltpu.PrefetchScalarGridSpec(
            num_scalar_prefetch=1,
            grid=(rows // block,),
            in_specs=[
                pl.BlockSpec((2, depth, block, lanes), lambda i, *_: (0, 0, i, 0)),
                pl.BlockSpec(memory_space=pl.ANY),
            ],
            out_specs=[
                pl.BlockSpec((2, block, depth, lanes), lambda i, *_: (0, i, 0, 0)),
                pl.BlockSpec((2, depth, lanes), lambda i, *_: (0, i, 0)),
            ],
        ),
        out_shape=[
            jax.ShapeDtypeStruct((2, rows, depth, lanes), jnp.float32),
            jax.ShapeDtypeStruct((2, depth * (rows // block), lanes), jnp.float32),
        ],
        interpret=INTERPRET,
        name="transfer_tables",
    )(upper.astype(jnp.int32).reshape(1), psf, after)
    first = first[:, :depth]
    pairs = [(0, space_count // 2), (space_count // 2, 0)]
    other = lax.ppermute(first, "space", pairs)
    change = jnp.where(special, 0.5 * (first - other), 0.0)
    column = jnp.where(upper, change[:, :, half], change[:, :, 0])[:, :, None]
    lane = lax.broadcasted_iota(jnp.int32, (depth, lanes), 1)
    cross = jnp.stack(
        [
            jnp.where(lane % half == 0, column[0], 0.0),
            jnp.where(lane == 0, -column[1], jnp.where(lane == half, column[1], 0.0)),
        ]
    )
    return main, cross


def send(array, axis, count, flip):
    if flip == 0:
        return array
    return lax.ppermute(array, axis, [(i, i ^ flip) for i in range(count)])


def shards(estimate, observed, valid, psf_spectrum):
    space_count = lax.axis_size("space")
    views = lax.axis_size("view")
    planes, row_total, lanes = estimate.shape
    depth = planes * space_count
    view_count = views * observed.shape[0]
    columns_f, columns_i = column_tables(lanes, 1.0 / (depth * row_total * lanes))
    rows_f, rows_i, masks_f, masks_i = row_tables(row_total, lanes)
    tables = {
        "forward": (jnp.asarray(columns_f), jnp.asarray(rows_f), jnp.asarray(masks_f)),
        "inverse": (jnp.asarray(columns_i), jnp.asarray(rows_i), jnp.asarray(masks_i)),
    }
    observed, valid = observed[0], valid[0]
    place = lax.axis_index("space")
    me = lax.axis_index("view")
    device = place.astype(jnp.int32).reshape(1)

    shared = planes % views == 0 and views & (views - 1) == 0
    blocks = views if shared else 1
    share = planes // blocks
    strides = [1 << bit for bit in range(blocks.bit_length() - 1)]
    flips = [0]
    for stride in reversed(strides):
        flips = flips + [f ^ stride for f in flips]
    half_space = space_count // 2
    groups = [list(range(half_space, space_count)), list(range(half_space))]
    chunk = planes // 2 if planes % 2 == 0 else planes
    chunks = range(0, planes, chunk)

    def plane_order(entries, count):
        starts = [(place ^ k) * planes + first for k, first in entries]
        return (jnp.stack(starts)[:, None] + jnp.arange(count, dtype=jnp.int32)[None, :]).reshape(-1)

    def first_of(flip):
        return (me ^ flip) * share if shared else 0

    own = lax.dynamic_slice_in_dim(estimate, me * share, share, 0) if shared else estimate
    spectrum = lateral_forward(own, device, tables, space_count)
    transfer = transfer_tables(psf_spectrum[0], spectrum[0], space_count)

    gathered_forward = depth_table(
        plane_order([(k, first_of(f)) for k in range(space_count) for f in flips], share), depth, False
    )
    shared_inverse = depth_table(
        plane_order([(k, first_of(f)) for f in flips for group in groups for k in group], share), depth, True
    )
    slab_entries = [[(k, start) for k in range(space_count)] for start in chunks]
    slab_forward = [depth_table(plane_order(e, chunk), depth, False) for e in slab_entries]
    slab_inverse = [depth_table(plane_order(e, chunk), depth, True) for e in slab_entries]

    def spread(pieces):
        moved = {k: send(pieces[k], "space", space_count, k) for k in reversed(range(space_count))}
        return [moved[k] for k in range(space_count)]

    for iteration in range(ITERS):
        last = iteration == ITERS - 1
        pieces = []
        for piece in spread(spectrum):
            copies = [piece]
            for stride in reversed(strides):
                copies = copies + [send(c, "view", views, stride) for c in copies]
            pieces += copies
        kept = None
        ratios = []
        for number, start in enumerate(chunks):
            final = number == len(chunks) - 1
            outs, stored = depth_step(
                pieces, kept, transfer, gathered_forward, slab_inverse[number],
                [chunk] * space_count, number == 0 and not final, False, depth,
            )
            pieces, kept = [], (stored if stored is not None else kept)
            ratios.append(ratio_step(spread(outs), observed, valid, start, device, tables))
        kept = None
        for number, ratio in enumerate(ratios):
            final = number == len(ratios) - 1
            counts = [share * len(group) for _ in flips for group in groups] if final else []
            outs, kept = depth_step(
                spread(ratio), kept, transfer, slab_forward[number], shared_inverse,
                counts, not final, True, depth,
            )
        summed = {}
        for number, group in enumerate(groups):
            parts = [outs[index * len(groups) + number] for index in range(blocks)]
            for stride in strides:
                middle = len(parts) // 2
                moved = [send(p, "view", views, stride) for p in parts[middle:]]
                if len(parts) == 2:
                    for index, k in enumerate(group):
                        window = slice(index * share, (index + 1) * share)
                        summed[k] = parts[0][window] + moved[0][window]
                parts = [kept_part + new for kept_part, new in zip(parts[:middle], moved)]
            if not shared:
                total = lax.psum(parts[0], "view")
                for index, k in enumerate(group):
                    summed[k] = total[index * share : (index + 1) * share]
            elif not strides:
                for index, k in enumerate(group):
                    summed[k] = parts[0][index * share : (index + 1) * share]
        own, spectrum = update_step(
            spread([summed[k] for k in range(space_count)]), own, float(view_count), device, tables, last
        )
    if not shared:
        return own
    copies = [own]
    for stride in reversed(strides):
        copies = copies + [send(c, "view", views, stride) for c in copies]
    refined = jnp.zeros_like(estimate)
    for flip, copy in zip(flips, copies):
        refined = lax.dynamic_update_slice_in_dim(refined, copy, first_of(flip), 0)
    return refined


def solution(mesh):
    return jax.shard_map(
        shards,
        mesh=mesh,
        in_specs=(
            P("space", "blocks", None),
            P("view", "space", "blocks", None),
            P("view", "space", "blocks", None),
            P("view", None, None, "space", None),
        ),
        out_specs=P("space", "blocks", None),
        check_vma=False,
    )
```

```python
import jax
import jax.numpy as jnp
import ml_dtypes
import numpy as np
from jax import lax
from jax.experimental import pallas as pl
from jax.experimental.pallas import tpu as pltpu
from jax.sharding import PartitionSpec as P

ITERS = 2
INTERPRET = False
VMEM_LIMIT = 16 * 2**20


def split_np(matrix):
    high = matrix.astype(ml_dtypes.bfloat16)
    low = (matrix - high.astype(np.float64)).astype(ml_dtypes.bfloat16)
    return high, low


def three_np(matrix):
    high, low = split_np(matrix)
    return np.concatenate([high, high, low], axis=1)


def angles_np(length):
    index = np.arange(length)
    return (np.outer(index, index) % length) * (2.0 * np.pi / length)


def column_tables(length, scale):
    half = length // 2
    angles = angles_np(length)
    cosines, sines = np.cos(angles), np.sin(angles)
    alternating = np.where(np.arange(length) % 2 == 0, 1.0, -1.0)
    forward = np.zeros((length, length))
    forward[:, :half] = cosines[:, :half]
    forward[:, half:] = -sines[:, :half]
    forward[:, half] = alternating
    inverse = np.zeros((length, length))
    inverse[:half] = 2.0 * cosines[:half]
    inverse[half:] = -2.0 * sines[:half]
    inverse[0] = 1.0
    inverse[half] = alternating
    inverse *= scale
    tables = []
    for matrix in (forward, inverse):
        high, low = split_np(matrix)
        both = np.concatenate([high, low], axis=1)
        tables.append(np.concatenate([both, both], axis=0))
    return tables


def row_tables(length, lanes):
    middle, half = length // 2, lanes // 2
    angles = angles_np(length)
    cosines, sines = np.cos(angles), np.sin(angles)
    sines[0] = -cosines[middle]
    sines[middle] = -cosines[0]
    forward = three_np(np.concatenate([cosines, sines], axis=0))
    inverse = three_np(np.concatenate([cosines.T, sines.T], axis=1))
    row = np.arange(length)[:, None]
    lane = np.arange(lanes)[None, :]
    plain = (lane % half) != 0
    lower = row < middle
    inner = (row % middle) != 0
    first, second = lane == 0, lane == half
    sign = np.where(lane < half, 1.0, -1.0)
    weight = np.where(inner, 2.0, 1.0)
    one = np.ones((length, lanes))
    forward_masks = np.stack(
        [
            one * (plain | (first & lower)),
            one * (first & ~lower),
            -one * (second & ~lower),
            sign * (plain & inner) - one * (second & lower),
        ]
    )
    inverse_masks = np.stack(
        [
            one * plain + weight * (first & lower),
            weight * (second & ~lower),
            -weight * (second & ~lower),
            -sign * (plain & inner) - weight * (first & lower),
        ]
    )
    return forward, inverse, forward_masks.astype(np.float32), inverse_masks.astype(np.float32)


def depth_tables(depth, order):
    angles = angles_np(depth)[:, order]
    forward = np.concatenate([np.cos(angles), np.sin(angles)], axis=0)
    inverse = np.concatenate([np.cos(angles.T), np.sin(angles.T)], axis=0)
    return jnp.asarray(three_np(forward)), jnp.asarray(three_np(inverse))


def split(value):
    high = value.astype(jnp.bfloat16)
    low = (value - high.astype(jnp.float32)).astype(jnp.bfloat16)
    return high, low


def three(value):
    high, low = split(value)
    return jnp.concatenate([high, low, high], axis=0)


def dot(left, right):
    return lax.dot_general(
        left, right, (((1,), (0,)), ((), ())), preferred_element_type=jnp.float32
    )


def along_columns(planes, columns):
    rows = planes[0].shape[0]
    value = dot(jnp.concatenate(split(jnp.concatenate(planes, axis=0)), axis=1), columns[...])
    lanes = value.shape[1] // 2
    value = value[:, :lanes] + value[:, lanes:]
    return [value[i * rows : (i + 1) * rows] for i in range(len(planes))]


def along_rows(planes, table):
    lanes = planes[0].shape[1]
    value = dot(table[...], three(jnp.concatenate(planes, axis=1)))
    return [value[:, i * lanes : (i + 1) * lanes] for i in range(len(planes))]


def planes_forward(planes, columns, rows, masks):
    spectra = []
    for both in along_rows(along_columns(planes, columns), rows):
        count, half = both.shape[0] // 2, both.shape[1] // 2
        cos_part, sin_part = both[:count], both[count:]
        spectra.append(
            cos_part * masks[0]
            + pltpu.roll(cos_part, half, 1) * masks[1]
            + sin_part * masks[2]
            + pltpu.roll(sin_part, half, 1) * masks[3]
        )
    return spectra


def planes_inverse(spectra, columns, rows, masks):
    sides = []
    for spectrum in spectra:
        rolled = pltpu.roll(spectrum, spectrum.shape[1] // 2, 1)
        sides.append(
            jnp.concatenate(
                [spectrum * masks[0] + rolled * masks[1], spectrum * masks[2] + rolled * masks[3]],
                axis=0,
            )
        )
    return along_columns(along_rows(sides, rows), columns)


VMEM = pl.BlockSpec(memory_space=pltpu.VMEM)
SMEM = pl.BlockSpec(memory_space=pltpu.SMEM)
ANY = pl.BlockSpec(memory_space=pl.ANY)


def flipped(ids_ref, axis, flip, count):
    return pl.multiple_of(jnp.bitwise_xor(ids_ref[axis], flip) * count, count)


def lateral_call(body, ids, operands, pieces, places, constants, shape, out_planes, out_places):
    planes, rows, lanes, part_rows = shape
    step = 2 if planes % 2 == 0 else 1

    def kernel(ids_ref, *refs):
        spans = np.cumsum(
            [0, len(operands), len(pieces), len(constants), out_planes, len(out_places), step, step]
        )
        groups = [refs[a:b] for a, b in zip(spans[:-1], spans[1:])]
        ins, piece_refs, constant_refs, plane_refs, out_refs, scratch_in, scratch_out = groups

        def row_range(place):
            k, first, count = place
            return pl.ds(pl.multiple_of(flipped(ids_ref, 0, k, part_rows) + first, count), count)

        def turn(number, carry):
            indices = [number * step + i for i in range(step)]

            def read():
                for i, index in enumerate(indices):
                    for place, ref in zip(places, piece_refs):
                        scratch_in[i][row_range(place), :] = ref[index]
                return [scratch[...] for scratch in scratch_in]

            def write(values):
                for i, index in enumerate(indices):
                    scratch_out[i][...] = values[i]
                    for place, ref in zip(out_places, out_refs):
                        ref[index] = scratch_out[i][row_range(place), :]

            body(indices, ins, read, constant_refs, plane_refs, write)
            return carry

        lax.fori_loop(0, planes // step, turn, 0)

    return pl.pallas_call(
        kernel,
        in_specs=[SMEM] + [VMEM] * (len(operands) + len(pieces) + len(constants)),
        out_specs=[VMEM] * (out_planes + len(out_places)),
        scratch_shapes=[pltpu.VMEM((rows, lanes), jnp.float32)] * (2 * step),
        out_shape=[jax.ShapeDtypeStruct((planes, rows, lanes), jnp.float32)] * out_planes
        + [jax.ShapeDtypeStruct((planes, place[2], lanes), jnp.float32) for place in out_places],
        interpret=INTERPRET,
        compiler_params=pltpu.CompilerParams(vmem_limit_bytes=VMEM_LIMIT),
    )(ids, *operands, *pieces, *constants)


def lateral_forward(volume, ids, tables, part_rows, out_places):
    def body(indices, ins, read, constants, _, write):
        write(planes_forward([ins[0][i] for i in indices], *constants))

    return lateral_call(
        body, ids, [volume], [], [], tables["forward"],
        volume.shape + (part_rows,), 0, out_places,
    )


def ratio_step(pieces, places, observed, valid, offset, ids, tables, part_rows, out_places):
    planes = pieces[0].shape[0]

    def body(indices, ins, read, constants, _, write):
        ratios = []
        for index, blurred in zip(indices, planes_inverse(read(), *constants[:3])):
            mask = ins[1][offset + index].astype(jnp.float32)
            ratios.append(mask * ins[0][offset + index] / blurred + (1.0 - mask))
        write(planes_forward(ratios, *constants[3:]))

    return lateral_call(
        body, ids, [observed, valid], pieces, places,
        tables["inverse"] + tables["forward"], (planes,) + observed.shape[1:] + (part_rows,), 0, out_places,
    )


def update_step(pieces, places, estimate, view_count, ids, tables, part_rows, out_places):
    last = not out_places

    def body(indices, ins, read, constants, outs, write):
        updated = []
        for index, combined in zip(indices, planes_inverse(read(), *constants[:3])):
            updated.append(ins[0][index] * combined / view_count)
            outs[0][index] = updated[-1]
        if not last:
            write(planes_forward(updated, *constants[3:]))

    constants = tables["inverse"] + (() if last else tables["forward"])
    results = lateral_call(
        body, ids, [estimate], pieces, places, constants,
        estimate.shape + (part_rows,), 1, out_places,
    )
    return results[0], results[1:]


BLOCK_ROWS = 8


def depth_step(ids, pieces, places, added, transfer, forward, inverse, outs, keep, adjoint, span, shape):
    main, cross = transfer
    _, _, depth, lanes = main.shape
    first_row, rows = shape
    half = lanes // 2
    block = BLOCK_ROWS
    in_count = forward.shape[1] // 3
    out_count = inverse.shape[0] // 2
    operands = list(pieces)
    if pieces:
        operands += [main, cross, forward]
    if added is not None:
        operands.append(added)
    if outs:
        operands.append(inverse)
    out_shape = [
        jax.ShapeDtypeStruct((sum(place[1] for place in places_), rows, lanes), jnp.float32)
        for places_ in outs
    ]
    if keep:
        out_shape.append(jax.ShapeDtypeStruct((rows, depth, lanes), jnp.float32))
    side = -1.0 if adjoint else 1.0
    scratch = []
    if pieces:
        scratch.append(pltpu.VMEM((in_count * rows, lanes), jnp.float32))
    if outs:
        scratch.append(pltpu.VMEM((out_count * rows, lanes), jnp.float32))

    def body(ids_ref, *refs):
        refs = list(refs)
        ins = [refs.pop(0) for _ in pieces]
        if pieces:
            main_ref, cross_ref, forward_ref = refs.pop(0), refs.pop(0), refs.pop(0)
        added_ref = refs.pop(0) if added is not None else None
        inverse_ref = refs.pop(0) if outs else None
        out_refs = [refs.pop(0) for _ in outs]
        keep_ref = refs.pop(0) if keep else None
        gathered = refs.pop(0) if pieces else None
        grown_out = refs.pop(0) if outs else None

        def planes_of(place, span):
            _, count, k, extra, flip, share = place
            start = flipped(ids_ref, 0, k, span) + extra
            if share:
                start = start + flipped(ids_ref, 1, flip, share)
            return lambda turn, total: pl.ds(
                pl.multiple_of((turn * total + start) * block, count * block), count * block
            )

        def sign(count):
            lane = lax.broadcasted_iota(jnp.int32, (count, lanes), 1)
            return jnp.where(lane < half, 1.0, -1.0)

        for ref, places_ in zip(ins, places):
            for place in places_:
                count = place[1]
                at = planes_of(place, span[0])
                for turn in range(rows // block):
                    gathered[at(turn, in_count), :] = ref[
                        place[0] : place[0] + count, turn * block : (turn + 1) * block
                    ].reshape(count * block, lanes)

        def some(turn, carry):
            for pair in range(block // 2):
                one_pair(turn, (2 * pair, 2 * pair + 1))
            return carry

        def one_pair(turn, lines):
            ks = [turn * block + line for line in lines]
            results = []
            if pieces:
                both = jnp.concatenate(
                    [
                        gathered[pl.ds(turn * in_count * block + line, in_count, stride=block), :]
                        for line in lines
                    ],
                    axis=1,
                )
                grown = dot(forward_ref[...], three(both))
                for index, k in enumerate(ks):
                    lanes_of = slice(index * lanes, (index + 1) * lanes)
                    cos_part, sin_part = grown[:depth, lanes_of], grown[depth:, lanes_of]
                    sin_roll = pltpu.roll(sin_part, half, 1)
                    spectrum = cos_part + sign(depth) * sin_roll
                    result = (
                        spectrum * main_ref[0, first_row + k]
                        + pltpu.roll(spectrum, half, 1) * (main_ref[1, first_row + k] * side)
                    )
                    if lines[index] == 0 and first_row == 0:
                        change = sign(depth) * cos_part - sin_roll - spectrum
                        extra = (
                            change * cross_ref[0]
                            + pltpu.roll(change, half, 1) * cross_ref[1] * side
                        )
                        result = result + jnp.where(turn == 0, extra, 0.0)
                    if added is not None:
                        result = result + added_ref[first_row + k]
                    results.append(result)
            else:
                results = [added_ref[first_row + k] for k in ks]
            if keep:
                for k, result in zip(ks, results):
                    keep_ref[k] = result
            if not outs:
                return
            grown = dot(inverse_ref[...], three(jnp.concatenate(results, axis=1)))
            for index, k in enumerate(ks):
                lanes_of = slice(index * lanes, (index + 1) * lanes)
                cos_part, sin_part = grown[:out_count, lanes_of], grown[out_count:, lanes_of]
                grown_out[
                    pl.ds(turn * out_count * block + lines[index], out_count, stride=block), :
                ] = cos_part - sign(
                    out_count
                ) * pltpu.roll(sin_part, half, 1)

        lax.fori_loop(0, rows // block, some, 0)
        for ref, places_ in zip(out_refs, outs):
            for place in places_:
                count = place[1]
                at = planes_of(place, span[1])
                for turn in range(rows // block):
                    ref[place[0] : place[0] + count, turn * block : (turn + 1) * block] = grown_out[
                        at(turn, out_count), :
                    ].reshape(count, block, lanes)

    results = pl.pallas_call(
        body,
        out_shape=out_shape,
        in_specs=[SMEM] + [VMEM] * len(operands),
        out_specs=[VMEM] * len(out_shape),
        scratch_shapes=scratch,
        interpret=INTERPRET,
        compiler_params=pltpu.CompilerParams(vmem_limit_bytes=VMEM_LIMIT),
        name="depth_step",
    )(ids, *operands)
    return results[: len(outs)], (results[-1] if keep else None)


def rows_of(ref, k):
    planes, count, lanes = ref.shape
    return ref.reshape(planes * count, lanes).at[pl.ds(k, planes, stride=count), :]


def cross_tables(first, space_count):
    _, depth, lanes = first.shape
    half = lanes // 2
    device = lax.axis_index("space")
    upper = device >= space_count // 2
    special = (device % (space_count // 2)) == 0
    other = lax.ppermute(first, "space", [(0, space_count // 2), (space_count // 2, 0)])
    change = jnp.where(special, 0.5 * (first - other), 0.0)
    column = jnp.where(upper, change[:, :, half], change[:, :, 0])[:, :, None]
    lane = lax.broadcasted_iota(jnp.int32, (depth, lanes), 1)
    return jnp.stack(
        [
            jnp.where(lane % half == 0, column[0], 0.0),
            jnp.where(lane == 0, -column[1], jnp.where(lane == half, column[1], 0.0)),
        ]
    )


def transfer_table(psf, after, ids, space_count):
    _, depth, rows, lanes = psf.shape
    half = lanes // 2
    block = BLOCK_ROWS

    def body(ids_ref, psf_ref, _, main_ref):
        lane = lax.broadcasted_iota(jnp.int32, (depth, lanes), 1)
        first_lanes = (lane % half == 0) & (ids_ref[0] >= space_count // 2)
        for k in range(block):
            for part in range(2):
                value = rows_of(psf_ref.at[part], k)[...]
                rolled = pltpu.roll(value, half, 1)
                doubled = jnp.where(lane < half, value, rolled)
                other = jnp.where(lane < half, rolled, value)
                packed = jnp.where(first_lanes, other, doubled)
                if part == 1:
                    packed = jnp.where(lane < half, -packed, packed)
                main_ref[part, k] = packed

    return pl.pallas_call(
        body,
        grid_spec=pltpu.PrefetchScalarGridSpec(
            num_scalar_prefetch=1,
            grid=(rows // block,),
            in_specs=[
                pl.BlockSpec((2, depth, block, lanes), lambda i, *_: (0, 0, i, 0)),
                pl.BlockSpec(memory_space=pl.ANY),
            ],
            out_specs=pl.BlockSpec((2, block, depth, lanes), lambda i, *_: (0, i, 0, 0)),
        ),
        out_shape=jax.ShapeDtypeStruct((2, rows, depth, lanes), jnp.float32),
        interpret=INTERPRET,
        compiler_params=pltpu.CompilerParams(vmem_limit_bytes=VMEM_LIMIT),
        name="transfer_table",
    )(ids, psf, after)


def send(array, axis, count, flip):
    if flip == 0:
        return array
    return lax.ppermute(array, axis, [(i, i ^ flip) for i in range(count)])


def join_planes(ids, copies, flips, planes):
    share, rows, lanes = copies[0].shape
    count = len(copies)

    def body(ids_ref, *refs):
        ins, out_ref, sems = refs[:count], refs[count], refs[count + 1]
        moves = [
            pltpu.make_async_copy(
                ref, out_ref.at[pl.ds(flipped(ids_ref, 1, flip, share), share)], sems.at[i]
            )
            for i, (ref, flip) in enumerate(zip(ins, flips))
        ]
        for move in moves:
            move.start()
        for move in moves:
            move.wait()

    return pl.pallas_call(
        body,
        out_shape=jax.ShapeDtypeStruct((planes, rows, lanes), jnp.float32),
        in_specs=[SMEM] + [ANY] * count,
        out_specs=ANY,
        scratch_shapes=[pltpu.SemaphoreType.DMA((count,))],
        interpret=INTERPRET,
        compiler_params=pltpu.CompilerParams(vmem_limit_bytes=VMEM_LIMIT),
        name="join_planes",
    )(ids, *copies)


def shards(estimate, observed, valid, psf_spectrum):
    space_count = lax.axis_size("space")
    views = lax.axis_size("view")
    planes, row_total, lanes = estimate.shape
    depth = planes * space_count
    part_rows = row_total // space_count
    view_count = views * observed.shape[0]
    columns_f, columns_i = column_tables(lanes, 1.0 / (depth * row_total * lanes))
    rows_f, rows_i, masks_f, masks_i = row_tables(row_total, lanes)
    tables = {
        "forward": (jnp.asarray(columns_f), jnp.asarray(rows_f), jnp.asarray(masks_f)),
        "inverse": (jnp.asarray(columns_i), jnp.asarray(rows_i), jnp.asarray(masks_i)),
    }
    observed, valid = observed[0], valid[0]
    ids = jnp.stack([lax.axis_index("space"), lax.axis_index("view")]).astype(jnp.int32)

    shared = planes % views == 0 and views & (views - 1) == 0
    blocks = views if shared else 1
    share = planes // blocks
    strides = [1 << bit for bit in range(blocks.bit_length() - 1)]
    flips = [0]
    for stride in reversed(strides):
        flips = flips + [f ^ stride for f in flips]
    ks = list(range(space_count))
    chunk = planes // 2 if planes % 2 == 0 else planes
    starts = list(range(0, planes, chunk))
    part = part_rows // 2 if part_rows % (2 * BLOCK_ROWS) == 0 else part_rows
    whole_rows = [(0, part_rows)]
    half_rows = [(first, part) for first in range(0, part_rows, part)]

    def row_places(ranges):
        return [(k, first, count) for first, count in ranges for k in ks]

    slabs = np.arange(space_count)[:, None] * planes
    full_tables = depth_tables(depth, np.arange(depth))
    chunk_tables = [
        depth_tables(depth, (slabs + start + np.arange(chunk)[None, :]).reshape(-1)) for start in starts
    ]
    chunk_places = [[(0, chunk, k, 0, 0, 0)] for k in ks]
    view_share = share if shared else 0

    cross = cross_tables(psf_spectrum[0, :, :, 0, :], space_count)
    own = lax.dynamic_slice_in_dim(estimate, ids[1] * share, share, 0) if shared else estimate
    spectrum = lateral_forward(own, ids, tables, part_rows, row_places(whole_rows))
    main = transfer_table(psf_spectrum[0], spectrum[0], ids, space_count)
    transfer = (main, cross)

    def spread(pieces):
        moved = {k: send(pieces[k], "space", space_count, k) for k in reversed(ks)}
        return [moved[k] for k in ks]

    for iteration in range(ITERS):
        last = iteration == ITERS - 1
        pieces, places = [], []
        for k, piece in enumerate(spread(spectrum)):
            copies = [piece]
            for stride in reversed(strides):
                copies = copies + [send(c, "view", views, stride) for c in copies]
            pieces += copies
            places += [[(0, share, k, 0, flip, view_share)] for flip in flips]
        outs, _ = depth_step(
            ids, pieces, places, None, transfer, full_tables[0], full_tables[1],
            [[(0, chunk, k, start, 0, 0)] for start in starts for k in ks],
            False, False, (planes, planes), (0, part_rows),
        )
        ratios = []
        for number, start in enumerate(starts):
            final = number == len(starts) - 1
            ratios.append(
                ratio_step(
                    spread(outs[number * space_count : (number + 1) * space_count]), row_places(whole_rows),
                    observed, valid, start, ids, tables, part_rows,
                    row_places(half_rows if final else whole_rows),
                )
            )
        kept = None
        for number, ratio in enumerate(ratios[:-1]):
            arrived = spread(ratio)
            _, kept = depth_step(
                ids, arrived, chunk_places, kept, transfer, chunk_tables[number][0], full_tables[1],
                [], True, True, (chunk, planes), (0, part_rows),
            )
        arrived = []
        for number in range(len(half_rows)):
            arrived.append(spread(ratios[-1][number * space_count : (number + 1) * space_count]))
        combined = []
        for number, shape in enumerate(half_rows):
            parts, _ = depth_step(
                ids, arrived[number], chunk_places, kept, transfer,
                chunk_tables[-1][0], full_tables[1],
                [[(k * share, share, k, 0, flip, view_share) for k in ks] for flip in flips],
                False, True, (chunk, planes), shape,
            )
            for stride in strides:
                middle = len(parts) // 2
                moved = [send(p, "view", views, stride) for p in parts[middle:]]
                if middle == 1:
                    parts = [parts[0][k * share : (k + 1) * share] + moved[0][k * share : (k + 1) * share] for k in ks]
                else:
                    parts = [own_part + new for own_part, new in zip(parts[:middle], moved)]
            if not strides:
                total = parts[0] if shared else lax.psum(parts[0], "view")
                parts = [total[k * share : (k + 1) * share] for k in ks]
            combined += spread(parts)
        own, spectrum = update_step(
            combined, row_places(half_rows), own, float(view_count), ids, tables, part_rows,
            [] if last else row_places(whole_rows),
        )
    if not shared:
        return own
    copies = [own]
    for stride in reversed(strides):
        copies = copies + [send(c, "view", views, stride) for c in copies]
    return join_planes(ids, copies, flips, planes)


def solution(mesh):
    return jax.shard_map(
        shards,
        mesh=mesh,
        in_specs=(
            P("space", "blocks", None),
            P("view", "space", "blocks", None),
            P("view", "space", "blocks", None),
            P("view", None, None, "space", None),
        ),
        out_specs=P("space", "blocks", None),
        check_vma=False,
    )
```

```python
import jax
import jax.numpy as jnp
import ml_dtypes
import numpy as np
from jax import lax
from jax.experimental import pallas as pl
from jax.experimental.pallas import tpu as pltpu
from jax.sharding import PartitionSpec as P

ITERS = 2
INTERPRET = False
VMEM_LIMIT = 16 * 2**20


def split_np(matrix):
    high = matrix.astype(ml_dtypes.bfloat16)
    low = (matrix - high.astype(np.float64)).astype(ml_dtypes.bfloat16)
    return high, low


def three_np(matrix):
    high, low = split_np(matrix)
    return np.concatenate([high, high, low], axis=1)


def angles_np(length):
    index = np.arange(length)
    return (np.outer(index, index) % length) * (2.0 * np.pi / length)


def column_tables(length, scale):
    half = length // 2
    angles = angles_np(length)
    cosines, sines = np.cos(angles), np.sin(angles)
    alternating = np.where(np.arange(length) % 2 == 0, 1.0, -1.0)
    forward = np.zeros((length, length))
    forward[:, :half] = cosines[:, :half]
    forward[:, half:] = -sines[:, :half]
    forward[:, half] = alternating
    inverse = np.zeros((length, length))
    inverse[:half] = 2.0 * cosines[:half]
    inverse[half:] = -2.0 * sines[:half]
    inverse[0] = 1.0
    inverse[half] = alternating
    inverse *= scale
    tables = []
    for matrix in (forward, inverse):
        high, low = split_np(matrix)
        both = np.concatenate([high, low], axis=1)
        tables.append(np.concatenate([both, both], axis=0))
    return tables


def row_tables(length, lanes):
    middle, half = length // 2, lanes // 2
    angles = angles_np(length)
    cosines, sines = np.cos(angles), np.sin(angles)
    sines[0] = -cosines[middle]
    sines[middle] = -cosines[0]
    forward = three_np(np.concatenate([cosines, sines], axis=0))
    inverse = three_np(np.concatenate([cosines.T, sines.T], axis=1))
    row = np.arange(length)[:, None]
    lane = np.arange(lanes)[None, :]
    plain = (lane % half) != 0
    lower = row < middle
    inner = (row % middle) != 0
    first, second = lane == 0, lane == half
    sign = np.where(lane < half, 1.0, -1.0)
    weight = np.where(inner, 2.0, 1.0)
    one = np.ones((length, lanes))
    forward_masks = np.stack(
        [
            one * (plain | (first & lower)),
            one * (first & ~lower),
            -one * (second & ~lower),
            sign * (plain & inner) - one * (second & lower),
        ]
    )
    inverse_masks = np.stack(
        [
            one * plain + weight * (first & lower),
            weight * (second & ~lower),
            -weight * (second & ~lower),
            -sign * (plain & inner) - weight * (first & lower),
        ]
    )
    return forward, inverse, forward_masks.astype(np.float32), inverse_masks.astype(np.float32)


def depth_tables(depth, order):
    angles = angles_np(depth)[:, order]
    forward = np.concatenate([np.cos(angles), np.sin(angles)], axis=0)
    inverse = np.concatenate([np.cos(angles.T), np.sin(angles.T)], axis=0)
    return jnp.asarray(three_np(forward)), jnp.asarray(three_np(inverse))


def split(value):
    high = value.astype(jnp.bfloat16)
    low = (value - high.astype(jnp.float32)).astype(jnp.bfloat16)
    return high, low


def three(value):
    high, low = split(value)
    return jnp.concatenate([high, low, high], axis=0)


def dot(left, right):
    return lax.dot_general(
        left, right, (((1,), (0,)), ((), ())), preferred_element_type=jnp.float32
    )


def along_columns(planes, columns):
    rows = planes[0].shape[0]
    value = dot(jnp.concatenate(split(jnp.concatenate(planes, axis=0)), axis=1), columns[...])
    lanes = value.shape[1] // 2
    value = value[:, :lanes] + value[:, lanes:]
    return [value[i * rows : (i + 1) * rows] for i in range(len(planes))]


def along_rows(planes, table):
    lanes = planes[0].shape[1]
    value = dot(table[...], three(jnp.concatenate(planes, axis=1)))
    return [value[:, i * lanes : (i + 1) * lanes] for i in range(len(planes))]


def planes_forward(planes, columns, rows, masks):
    spectra = []
    for both in along_rows(along_columns(planes, columns), rows):
        count, half = both.shape[0] // 2, both.shape[1] // 2
        cos_part, sin_part = both[:count], both[count:]
        spectra.append(
            cos_part * masks[0]
            + pltpu.roll(cos_part, half, 1) * masks[1]
            + sin_part * masks[2]
            + pltpu.roll(sin_part, half, 1) * masks[3]
        )
    return spectra


def planes_inverse(spectra, columns, rows, masks):
    sides = []
    for spectrum in spectra:
        rolled = pltpu.roll(spectrum, spectrum.shape[1] // 2, 1)
        sides.append(
            jnp.concatenate(
                [spectrum * masks[0] + rolled * masks[1], spectrum * masks[2] + rolled * masks[3]],
                axis=0,
            )
        )
    return along_columns(along_rows(sides, rows), columns)


VMEM = pl.BlockSpec(memory_space=pltpu.VMEM)
SMEM = pl.BlockSpec(memory_space=pltpu.SMEM)
ANY = pl.BlockSpec(memory_space=pl.ANY)


def flipped(ids_ref, axis, flip, count):
    return pl.multiple_of(jnp.bitwise_xor(ids_ref[axis], flip) * count, count)


def lateral_call(body, ids, operands, pieces, places, constants, shape, out_planes, out_places):
    planes, rows, lanes, part_rows = shape
    step = 2 if planes % 2 == 0 else 1

    def kernel(ids_ref, *refs):
        spans = np.cumsum(
            [0, len(operands), len(pieces), len(constants), out_planes, len(out_places), step, step]
        )
        groups = [refs[a:b] for a, b in zip(spans[:-1], spans[1:])]
        ins, piece_refs, constant_refs, plane_refs, out_refs, scratch_in, scratch_out = groups

        def row_range(place):
            k, first, count = place
            return pl.ds(pl.multiple_of(flipped(ids_ref, 0, k, part_rows) + first, count), count)

        def turn(number, carry):
            indices = [number * step + i for i in range(step)]

            def read():
                for i, index in enumerate(indices):
                    for place, ref in zip(places, piece_refs):
                        scratch_in[i][row_range(place), :] = ref[index]
                return [scratch[...] for scratch in scratch_in]

            def write(values):
                for i, index in enumerate(indices):
                    scratch_out[i][...] = values[i]
                    for place, ref in zip(out_places, out_refs):
                        ref[index] = scratch_out[i][row_range(place), :]

            body(indices, ins, read, constant_refs, plane_refs, write)
            return carry

        lax.fori_loop(0, planes // step, turn, 0)

    return pl.pallas_call(
        kernel,
        in_specs=[SMEM] + [VMEM] * (len(operands) + len(pieces) + len(constants)),
        out_specs=[VMEM] * (out_planes + len(out_places)),
        scratch_shapes=[pltpu.VMEM((rows, lanes), jnp.float32)] * (2 * step),
        out_shape=[jax.ShapeDtypeStruct((planes, rows, lanes), jnp.float32)] * out_planes
        + [jax.ShapeDtypeStruct((planes, place[2], lanes), jnp.float32) for place in out_places],
        interpret=INTERPRET,
        compiler_params=pltpu.CompilerParams(vmem_limit_bytes=VMEM_LIMIT),
    )(ids, *operands, *pieces, *constants)


def lateral_forward(volume, ids, tables, part_rows, out_places):
    def body(indices, ins, read, constants, _, write):
        write(planes_forward([ins[0][i] for i in indices], *constants))

    return lateral_call(
        body, ids, [volume], [], [], tables["forward"],
        volume.shape + (part_rows,), 0, out_places,
    )


def ratio_step(pieces, places, observed, valid, offset, ids, tables, part_rows, out_places):
    planes = pieces[0].shape[0]

    def body(indices, ins, read, constants, _, write):
        ratios = []
        for index, blurred in zip(indices, planes_inverse(read(), *constants[:3])):
            mask = ins[1][offset + index].astype(jnp.float32)
            ratios.append(mask * ins[0][offset + index] / blurred + (1.0 - mask))
        write(planes_forward(ratios, *constants[3:]))

    return lateral_call(
        body, ids, [observed, valid], pieces, places,
        tables["inverse"] + tables["forward"], (planes,) + observed.shape[1:] + (part_rows,), 0, out_places,
    )


def update_step(pieces, places, estimate, view_count, ids, tables, part_rows, out_places):
    last = not out_places

    def body(indices, ins, read, constants, outs, write):
        updated = []
        for index, combined in zip(indices, planes_inverse(read(), *constants[:3])):
            updated.append(ins[0][index] * combined / view_count)
            outs[0][index] = updated[-1]
        if not last:
            write(planes_forward(updated, *constants[3:]))

    constants = tables["inverse"] + (() if last else tables["forward"])
    results = lateral_call(
        body, ids, [estimate], pieces, places, constants,
        estimate.shape + (part_rows,), 1, out_places,
    )
    return results[0], results[1:]


BLOCK_ROWS = 8


def depth_step(ids, pieces, places, added, transfer, forward, inverse, outs, keep, adjoint, span, shape, raw=0):
    main, cross = transfer
    depth, lanes = cross.shape[1:]
    first_row, rows = shape
    half = lanes // 2
    block = BLOCK_ROWS
    in_count = forward.shape[1] // 3
    out_count = inverse.shape[0] // 2
    operands = list(pieces)
    if pieces:
        operands += [main, cross, forward]
    if added is not None:
        operands.append(added)
    if outs:
        operands.append(inverse)
    out_shape = [
        jax.ShapeDtypeStruct((sum(place[1] for place in places_), rows, lanes), jnp.float32)
        for places_ in outs
    ]
    if keep:
        out_shape.append(jax.ShapeDtypeStruct((rows, depth, lanes), jnp.float32))
    side = -1.0 if adjoint else 1.0
    scratch = []
    if pieces:
        scratch.append(pltpu.VMEM((in_count * rows, lanes), jnp.float32))
    if outs:
        scratch.append(pltpu.VMEM((out_count * rows, lanes), jnp.float32))
    if raw:
        scratch.append(pltpu.VMEM((2 * depth * block, lanes), jnp.float32))

    def body(ids_ref, *refs):
        refs = list(refs)
        ins = [refs.pop(0) for _ in pieces]
        if pieces:
            main_ref, cross_ref, forward_ref = refs.pop(0), refs.pop(0), refs.pop(0)
        added_ref = refs.pop(0) if added is not None else None
        inverse_ref = refs.pop(0) if outs else None
        out_refs = [refs.pop(0) for _ in outs]
        keep_ref = refs.pop(0) if keep else None
        gathered = refs.pop(0) if pieces else None
        grown_out = refs.pop(0) if outs else None
        raw_rows = refs.pop(0) if raw else None

        def planes_of(place, span):
            _, count, k, extra, flip, share = place
            start = flipped(ids_ref, 0, k, span) + extra
            if share:
                start = start + flipped(ids_ref, 1, flip, share)
            return lambda turn, total: pl.ds(
                pl.multiple_of((turn * total + start) * block, count * block), count * block
            )

        def sign(count):
            lane = lax.broadcasted_iota(jnp.int32, (count, lanes), 1)
            return jnp.where(lane < half, 1.0, -1.0)

        for ref, places_ in zip(ins, places):
            for place in places_:
                count = place[1]
                at = planes_of(place, span[0])
                for turn in range(rows // block):
                    row = turn * block + (first_row if ref.shape[1] > rows else 0)
                    gathered[at(turn, in_count), :] = ref[
                        place[0] : place[0] + count, row : row + block
                    ].reshape(count * block, lanes)

        def main_of(part, turn, line):
            if not raw:
                return main_ref[part, first_row + turn * block + line]
            value = raw_rows[pl.ds(part * depth * block + line, depth, stride=block), :]
            return pack_transfer(value, part, ids_ref[0] >= raw // 2)

        def some(turn, carry):
            if raw:
                row = pl.multiple_of(first_row + turn * block, block)
                raw_rows[...] = main_ref[:, :, pl.ds(row, block), :].reshape(2 * depth * block, lanes)
            for pair in range(block // 2):
                one_pair(turn, (2 * pair, 2 * pair + 1))
            return carry

        def one_pair(turn, lines):
            ks = [turn * block + line for line in lines]
            results = []
            if pieces:
                both = jnp.concatenate(
                    [
                        gathered[pl.ds(turn * in_count * block + line, in_count, stride=block), :]
                        for line in lines
                    ],
                    axis=1,
                )
                grown = dot(forward_ref[...], three(both))
                for index, k in enumerate(ks):
                    lanes_of = slice(index * lanes, (index + 1) * lanes)
                    cos_part, sin_part = grown[:depth, lanes_of], grown[depth:, lanes_of]
                    sin_roll = pltpu.roll(sin_part, half, 1)
                    spectrum = cos_part + sign(depth) * sin_roll
                    result = (
                        spectrum * main_of(0, turn, lines[index])
                        + pltpu.roll(spectrum, half, 1) * (main_of(1, turn, lines[index]) * side)
                    )
                    if lines[index] == 0 and first_row == 0:
                        change = sign(depth) * cos_part - sin_roll - spectrum
                        extra = (
                            change * cross_ref[0]
                            + pltpu.roll(change, half, 1) * cross_ref[1] * side
                        )
                        result = result + jnp.where(turn == 0, extra, 0.0)
                    if added is not None:
                        result = result + added_ref[first_row + k]
                    results.append(result)
            else:
                results = [added_ref[first_row + k] for k in ks]
            if keep:
                for k, result in zip(ks, results):
                    keep_ref[k] = result
            if not outs:
                return
            grown = dot(inverse_ref[...], three(jnp.concatenate(results, axis=1)))
            for index, k in enumerate(ks):
                lanes_of = slice(index * lanes, (index + 1) * lanes)
                cos_part, sin_part = grown[:out_count, lanes_of], grown[out_count:, lanes_of]
                grown_out[
                    pl.ds(turn * out_count * block + lines[index], out_count, stride=block), :
                ] = cos_part - sign(
                    out_count
                ) * pltpu.roll(sin_part, half, 1)

        lax.fori_loop(0, rows // block, some, 0)
        for ref, places_ in zip(out_refs, outs):
            for place in places_:
                count = place[1]
                at = planes_of(place, span[1])
                for turn in range(rows // block):
                    ref[place[0] : place[0] + count, turn * block : (turn + 1) * block] = grown_out[
                        at(turn, out_count), :
                    ].reshape(count, block, lanes)

    results = pl.pallas_call(
        body,
        out_shape=out_shape,
        in_specs=[SMEM] + [VMEM] * len(operands),
        out_specs=[VMEM] * len(out_shape),
        scratch_shapes=scratch,
        interpret=INTERPRET,
        compiler_params=pltpu.CompilerParams(vmem_limit_bytes=VMEM_LIMIT),
        name="depth_step",
    )(ids, *operands)
    return results[: len(outs)], (results[-1] if keep else None)


def rows_of(ref, k):
    planes, count, lanes = ref.shape
    return ref.reshape(planes * count, lanes).at[pl.ds(k, planes, stride=count), :]


def cross_tables(first, space_count):
    _, depth, lanes = first.shape
    half = lanes // 2
    device = lax.axis_index("space")
    upper = device >= space_count // 2
    special = (device % (space_count // 2)) == 0
    other = lax.ppermute(first, "space", [(0, space_count // 2), (space_count // 2, 0)])
    change = jnp.where(special, 0.5 * (first - other), 0.0)
    column = jnp.where(upper, change[:, :, half], change[:, :, 0])[:, :, None]
    lane = lax.broadcasted_iota(jnp.int32, (depth, lanes), 1)
    return jnp.stack(
        [
            jnp.where(lane % half == 0, column[0], 0.0),
            jnp.where(lane == 0, -column[1], jnp.where(lane == half, column[1], 0.0)),
        ]
    )


def pack_transfer(value, part, upper):
    lanes = value.shape[1]
    half = lanes // 2
    lane = lax.broadcasted_iota(jnp.int32, value.shape, 1)
    rolled = pltpu.roll(value, half, 1)
    low = lane < half
    first_lanes = jnp.where(upper, lane, 1) % half == 0
    packed = jnp.where(low ^ first_lanes, value, rolled)
    return packed if part == 0 else jnp.where(low, -packed, packed)


def transfer_table(psf, after, ids, space_count):
    _, depth, rows, lanes = psf.shape
    block = BLOCK_ROWS

    def body(ids_ref, psf_ref, _, main_ref):
        upper = ids_ref[0] >= space_count // 2
        for k in range(block):
            for part in range(2):
                main_ref[part, k] = pack_transfer(rows_of(psf_ref.at[part], k)[...], part, upper)

    return pl.pallas_call(
        body,
        grid_spec=pltpu.PrefetchScalarGridSpec(
            num_scalar_prefetch=1,
            grid=(rows // block,),
            in_specs=[
                pl.BlockSpec((2, depth, block, lanes), lambda i, *_: (0, 0, i, 0)),
                pl.BlockSpec(memory_space=pl.ANY),
            ],
            out_specs=pl.BlockSpec((2, block, depth, lanes), lambda i, *_: (0, i, 0, 0)),
        ),
        out_shape=jax.ShapeDtypeStruct((2, rows, depth, lanes), jnp.float32),
        interpret=INTERPRET,
        compiler_params=pltpu.CompilerParams(vmem_limit_bytes=VMEM_LIMIT),
        name="transfer_table",
    )(ids, psf, after)


def send(array, axis, count, flip):
    if flip == 0:
        return array
    return lax.ppermute(array, axis, [(i, i ^ flip) for i in range(count)])


def add_moved(parts, moved, size, share):
    sums, first = [], 0
    for part in parts:
        count = part.shape[0] // size
        new = moved[first * size : (first + count) * size]
        first += count
        if share:
            sums += [part[i : i + share] + new[i : i + share] for i in range(0, size, share)]
        else:
            sums.append(part + new)
    return sums


def join_planes(ids, copies, flips, planes):
    share, rows, lanes = copies[0].shape
    count = len(copies)

    def body(ids_ref, *refs):
        ins, out_ref, sems = refs[:count], refs[count], refs[count + 1]
        moves = [
            pltpu.make_async_copy(
                ref, out_ref.at[pl.ds(flipped(ids_ref, 1, flip, share), share)], sems.at[i]
            )
            for i, (ref, flip) in enumerate(zip(ins, flips))
        ]
        for move in moves:
            move.start()
        for move in moves:
            move.wait()

    return pl.pallas_call(
        body,
        out_shape=jax.ShapeDtypeStruct((planes, rows, lanes), jnp.float32),
        in_specs=[SMEM] + [ANY] * count,
        out_specs=ANY,
        scratch_shapes=[pltpu.SemaphoreType.DMA((count,))],
        interpret=INTERPRET,
        compiler_params=pltpu.CompilerParams(vmem_limit_bytes=VMEM_LIMIT),
        name="join_planes",
    )(ids, *copies)


def shards(estimate, observed, valid, psf_spectrum):
    space_count = lax.axis_size("space")
    views = lax.axis_size("view")
    planes, row_total, lanes = estimate.shape
    depth = planes * space_count
    part_rows = row_total // space_count
    view_count = views * observed.shape[0]
    columns_f, columns_i = column_tables(lanes, 1.0 / (depth * row_total * lanes))
    rows_f, rows_i, masks_f, masks_i = row_tables(row_total, lanes)
    tables = {
        "forward": (jnp.asarray(columns_f), jnp.asarray(rows_f), jnp.asarray(masks_f)),
        "inverse": (jnp.asarray(columns_i), jnp.asarray(rows_i), jnp.asarray(masks_i)),
    }
    observed, valid = observed[0], valid[0]
    ids = jnp.stack([lax.axis_index("space"), lax.axis_index("view")]).astype(jnp.int32)

    shared = planes % views == 0 and views & (views - 1) == 0
    blocks = views if shared else 1
    share = planes // blocks
    strides = [1 << bit for bit in range(blocks.bit_length() - 1)]
    flips = [0]
    for stride in reversed(strides):
        flips = flips + [f ^ stride for f in flips]
    ks = list(range(space_count))
    chunk = planes // 2 if planes % 2 == 0 else planes
    starts = list(range(0, planes, chunk))
    part = part_rows // 2 if part_rows % (2 * BLOCK_ROWS) == 0 else part_rows
    whole_rows = [(0, part_rows)]
    sum_groups = [flips[:1]] + [flips[1 << bit : 2 << bit] for bit in range(len(strides))]
    half_rows = [(first, part) for first in range(0, part_rows, part)]

    def row_places(ranges):
        return [(k, first, count) for first, count in ranges for k in ks]

    slabs = np.arange(space_count)[:, None] * planes
    full_tables = depth_tables(depth, np.arange(depth))
    chunk_tables = [
        depth_tables(depth, (slabs + start + np.arange(chunk)[None, :]).reshape(-1)) for start in starts
    ]
    chunk_places = [[(0, chunk, k, 0, 0, 0)] for k in ks]
    view_share = share if shared else 0

    cross = cross_tables(psf_spectrum[0, :, :, 0, :], space_count)
    own = lax.dynamic_slice_in_dim(estimate, ids[1] * share, share, 0) if shared else estimate
    spectrum = lateral_forward(own, ids, tables, part_rows, row_places(whole_rows))
    transfer = (psf_spectrum[0], cross)

    def spread(pieces):
        moved = {k: send(pieces[k], "space", space_count, k) for k in reversed(ks)}
        return [moved[k] for k in ks]

    for iteration in range(ITERS):
        last = iteration == ITERS - 1
        pieces, places = [], []
        arrived = spread(spectrum)
        for k, piece in enumerate(arrived):
            copies = [piece]
            for stride in reversed(strides):
                copies = copies + [send(c, "view", views, stride) for c in copies]
            pieces += copies
            places += [[(0, share, k, 0, flip, view_share)] for flip in flips]
        blurred = [[] for _ in starts]
        for shape in half_rows:
            outs, _ = depth_step(
                ids, pieces, places, None, transfer, full_tables[0], full_tables[1],
                [[(0, chunk, k, start, 0, 0)] for start in starts for k in ks],
                False, False, (planes, planes), shape, 0 if iteration else space_count,
            )
            for number in range(len(starts)):
                blurred[number] += spread(outs[number * space_count : (number + 1) * space_count])
        if iteration == 0:
            transfer = (transfer_table(psf_spectrum[0], outs[0], ids, space_count), cross)
        ratios = []
        for number, start in enumerate(starts):
            final = number == len(starts) - 1
            ratios.append(
                ratio_step(
                    blurred[number], row_places(half_rows), observed, valid, start, ids, tables, part_rows,
                    row_places(half_rows if final else whole_rows),
                )
            )
        kept = None
        for number, ratio in enumerate(ratios[:-1]):
            arrived = spread(ratio)
            _, kept = depth_step(
                ids, arrived, chunk_places, kept, transfer, chunk_tables[number][0], full_tables[1],
                [], True, True, (chunk, planes), (0, part_rows),
            )
        arrived = []
        for number in range(len(half_rows)):
            arrived.append(spread(ratios[-1][number * space_count : (number + 1) * space_count]))
        combined = []
        for number, shape in enumerate(half_rows):
            parts, _ = depth_step(
                ids, arrived[number], chunk_places, kept, transfer,
                chunk_tables[-1][0], full_tables[1],
                [
                    [
                        (k * share + index * share * space_count, share, k, 0, flip, view_share)
                        for index, flip in enumerate(group)
                        for k in ks
                    ]
                    for group in sum_groups
                ],
                False, True, (chunk, planes), shape,
            )
            for stride, group in zip(strides, reversed(sum_groups)):
                moved = send(parts[-1], "view", views, stride)
                parts = add_moved(parts[:-1], moved, space_count * share, share if len(parts) == 2 else 0)
            if not strides:
                total = parts[0] if shared else lax.psum(parts[0], "view")
                parts = [total[k * share : (k + 1) * share] for k in ks]
            combined += spread(parts)
        own, spectrum = update_step(
            combined, row_places(half_rows), own, float(view_count), ids, tables, part_rows,
            [] if last else row_places(whole_rows),
        )
    if not shared:
        return own
    copies = [own]
    for stride in reversed(strides):
        copies = copies + [send(c, "view", views, stride) for c in copies]
    return join_planes(ids, copies, flips, planes)


def solution(mesh):
    return jax.shard_map(
        shards,
        mesh=mesh,
        in_specs=(
            P("space", "blocks", None),
            P("view", "space", "blocks", None),
            P("view", "space", "blocks", None),
            P("view", None, None, "space", None),
        ),
        out_specs=P("space", "blocks", None),
        check_vma=False,
    )
```

```python
import jax
import jax.numpy as jnp
import ml_dtypes
import numpy as np
from jax import lax
from jax.experimental import pallas as pl
from jax.experimental.pallas import tpu as pltpu
from jax.sharding import PartitionSpec as P

ITERS = 2
INTERPRET = False
VMEM_LIMIT = 16 * 2**20


def split_np(matrix):
    high = matrix.astype(ml_dtypes.bfloat16)
    low = (matrix - high.astype(np.float64)).astype(ml_dtypes.bfloat16)
    return high, low


def three_np(matrix):
    high, low = split_np(matrix)
    return np.concatenate([high, high, low], axis=1)


def angles_np(length):
    index = np.arange(length)
    return (np.outer(index, index) % length) * (2.0 * np.pi / length)


def column_tables(length, scale):
    half = length // 2
    angles = angles_np(length)
    cosines, sines = np.cos(angles), np.sin(angles)
    alternating = np.where(np.arange(length) % 2 == 0, 1.0, -1.0)
    forward = np.zeros((length, length))
    forward[:, :half] = cosines[:, :half]
    forward[:, half:] = -sines[:, :half]
    forward[:, half] = alternating
    inverse = np.zeros((length, length))
    inverse[:half] = 2.0 * cosines[:half]
    inverse[half:] = -2.0 * sines[:half]
    inverse[0] = 1.0
    inverse[half] = alternating
    inverse *= scale
    tables = []
    for matrix in (forward, inverse):
        high, low = split_np(matrix)
        both = np.concatenate([high, low], axis=1)
        tables.append(np.concatenate([both, both], axis=0))
    return tables


def row_tables(length, lanes):
    middle, half = length // 2, lanes // 2
    angles = angles_np(length)
    cosines, sines = np.cos(angles), np.sin(angles)
    sines[0] = -cosines[middle]
    sines[middle] = -cosines[0]
    forward = three_np(np.concatenate([cosines, sines], axis=0))
    inverse = three_np(np.concatenate([cosines.T, sines.T], axis=1))
    row = np.arange(length)[:, None]
    lane = np.arange(lanes)[None, :]
    plain = (lane % half) != 0
    lower = row < middle
    inner = (row % middle) != 0
    first, second = lane == 0, lane == half
    sign = np.where(lane < half, 1.0, -1.0)
    weight = np.where(inner, 2.0, 1.0)
    one = np.ones((length, lanes))
    forward_masks = np.stack(
        [
            one * (plain | (first & lower)),
            one * (first & ~lower),
            -one * (second & ~lower),
            sign * (plain & inner) - one * (second & lower),
        ]
    )
    inverse_masks = np.stack(
        [
            one * plain + weight * (first & lower),
            weight * (second & ~lower),
            -weight * (second & ~lower),
            -sign * (plain & inner) - weight * (first & lower),
        ]
    )
    return forward, inverse, forward_masks.astype(np.float32), inverse_masks.astype(np.float32)


def depth_tables(depth, order):
    angles = angles_np(depth)[:, order]
    forward = np.concatenate([np.cos(angles), np.sin(angles)], axis=0)
    inverse = np.concatenate([np.cos(angles.T), np.sin(angles.T)], axis=0)
    return jnp.asarray(three_np(forward)), jnp.asarray(three_np(inverse))


def split(value):
    high = value.astype(jnp.bfloat16)
    low = (value - high.astype(jnp.float32)).astype(jnp.bfloat16)
    return high, low


def three(value):
    high, low = split(value)
    return jnp.concatenate([high, low, high], axis=0)


def dot(left, right):
    return lax.dot_general(
        left, right, (((1,), (0,)), ((), ())), preferred_element_type=jnp.float32
    )


def along_columns(planes, columns):
    rows = planes[0].shape[0]
    value = dot(jnp.concatenate(split(jnp.concatenate(planes, axis=0)), axis=1), columns[...])
    lanes = value.shape[1] // 2
    value = value[:, :lanes] + value[:, lanes:]
    return [value[i * rows : (i + 1) * rows] for i in range(len(planes))]


def along_rows(planes, table):
    lanes = planes[0].shape[1]
    value = dot(table[...], three(jnp.concatenate(planes, axis=1)))
    return [value[:, i * lanes : (i + 1) * lanes] for i in range(len(planes))]


def planes_forward(planes, columns, rows, masks):
    spectra = []
    for both in along_rows(along_columns(planes, columns), rows):
        count, half = both.shape[0] // 2, both.shape[1] // 2
        cos_part, sin_part = both[:count], both[count:]
        spectra.append(
            cos_part * masks[0]
            + pltpu.roll(cos_part, half, 1) * masks[1]
            + sin_part * masks[2]
            + pltpu.roll(sin_part, half, 1) * masks[3]
        )
    return spectra


def planes_inverse(spectra, columns, rows, masks):
    sides = []
    for spectrum in spectra:
        rolled = pltpu.roll(spectrum, spectrum.shape[1] // 2, 1)
        sides.append(
            jnp.concatenate(
                [spectrum * masks[0] + rolled * masks[1], spectrum * masks[2] + rolled * masks[3]],
                axis=0,
            )
        )
    return along_columns(along_rows(sides, rows), columns)


VMEM = pl.BlockSpec(memory_space=pltpu.VMEM)
SMEM = pl.BlockSpec(memory_space=pltpu.SMEM)
ANY = pl.BlockSpec(memory_space=pl.ANY)


def flipped(ids_ref, axis, flip, count):
    return pl.multiple_of(jnp.bitwise_xor(ids_ref[axis], flip) * count, count)


def lateral_call(body, ids, operands, pieces, places, constants, shape, out_planes, out_places):
    planes, rows, lanes, part_rows = shape
    step = 2 if planes % 2 == 0 else 1

    def kernel(ids_ref, *refs):
        spans = np.cumsum(
            [0, len(operands), len(pieces), len(constants), out_planes, len(out_places), step, step]
        )
        groups = [refs[a:b] for a, b in zip(spans[:-1], spans[1:])]
        ins, piece_refs, constant_refs, plane_refs, out_refs, scratch_in, scratch_out = groups

        def row_range(place):
            k, first, count = place
            start = flipped(ids_ref, 0, k, part_rows) + first
            return pl.ds(pl.multiple_of(start, BLOCK_ROWS), count)

        def turn(number, carry):
            indices = [number * step + i for i in range(step)]

            def read():
                for i, index in enumerate(indices):
                    for place, ref in zip(places, piece_refs):
                        scratch_in[i][row_range(place), :] = ref[index]
                return [scratch[...] for scratch in scratch_in]

            def write(values):
                for i, index in enumerate(indices):
                    scratch_out[i][...] = values[i]
                    for place, ref in zip(out_places, out_refs):
                        ref[index] = scratch_out[i][row_range(place), :]

            body(indices, ins, read, constant_refs, plane_refs, write)
            return carry

        lax.fori_loop(0, planes // step, turn, 0)

    return pl.pallas_call(
        kernel,
        in_specs=[SMEM] + [VMEM] * (len(operands) + len(pieces) + len(constants)),
        out_specs=[VMEM] * (out_planes + len(out_places)),
        scratch_shapes=[pltpu.VMEM((rows, lanes), jnp.float32)] * (2 * step),
        out_shape=[jax.ShapeDtypeStruct((planes, rows, lanes), jnp.float32)] * out_planes
        + [jax.ShapeDtypeStruct((planes, place[2], lanes), jnp.float32) for place in out_places],
        interpret=INTERPRET,
        compiler_params=pltpu.CompilerParams(vmem_limit_bytes=VMEM_LIMIT),
    )(ids, *operands, *pieces, *constants)


def lateral_forward(volume, ids, tables, part_rows, out_places):
    def body(indices, ins, read, constants, _, write):
        write(planes_forward([ins[0][i] for i in indices], *constants))

    return lateral_call(
        body, ids, [volume], [], [], tables["forward"],
        volume.shape + (part_rows,), 0, out_places,
    )


def ratio_step(pieces, places, observed, valid, offset, ids, tables, part_rows, out_places):
    planes = pieces[0].shape[0]

    def body(indices, ins, read, constants, _, write):
        ratios = []
        for index, blurred in zip(indices, planes_inverse(read(), *constants[:3])):
            mask = ins[1][offset + index].astype(jnp.float32)
            ratios.append(mask * ins[0][offset + index] / blurred + (1.0 - mask))
        write(planes_forward(ratios, *constants[3:]))

    return lateral_call(
        body, ids, [observed, valid], pieces, places,
        tables["inverse"] + tables["forward"], (planes,) + observed.shape[1:] + (part_rows,), 0, out_places,
    )


def update_step(pieces, places, estimate, view_count, ids, tables, part_rows, out_places):
    last = not out_places

    def body(indices, ins, read, constants, outs, write):
        updated = []
        for index, combined in zip(indices, planes_inverse(read(), *constants[:3])):
            updated.append(ins[0][index] * combined / view_count)
            outs[0][index] = updated[-1]
        if not last:
            write(planes_forward(updated, *constants[3:]))

    constants = tables["inverse"] + (() if last else tables["forward"])
    results = lateral_call(
        body, ids, [estimate], pieces, places, constants,
        estimate.shape + (part_rows,), 1, out_places,
    )
    return results[0], results[1:]


BLOCK_ROWS = 8


def depth_step(ids, pieces, places, added, transfer, forward, inverse, outs, keep, adjoint, span, shape, raw=0):
    main, cross = transfer
    depth, lanes = cross.shape[1:]
    first_row, rows = shape
    half = lanes // 2
    block = BLOCK_ROWS
    in_count = forward.shape[1] // 3
    out_count = inverse.shape[0] // 2
    operands = list(pieces)
    if pieces:
        operands += [main, cross, forward]
    if added is not None:
        operands.append(added)
    if outs:
        operands.append(inverse)
    out_shape = [
        jax.ShapeDtypeStruct((sum(place[1] for place in places_), rows, lanes), jnp.float32)
        for places_ in outs
    ]
    if keep:
        out_shape.append(jax.ShapeDtypeStruct((rows, depth, lanes), jnp.float32))
    side = -1.0 if adjoint else 1.0
    scratch = []
    if pieces:
        scratch.append(pltpu.VMEM((in_count * rows, lanes), jnp.float32))
    if outs:
        scratch.append(pltpu.VMEM((out_count * rows, lanes), jnp.float32))
    if raw:
        scratch.append(pltpu.VMEM((2 * depth * block, lanes), jnp.float32))

    def body(ids_ref, *refs):
        refs = list(refs)
        ins = [refs.pop(0) for _ in pieces]
        if pieces:
            main_ref, cross_ref, forward_ref = refs.pop(0), refs.pop(0), refs.pop(0)
        added_ref = refs.pop(0) if added is not None else None
        inverse_ref = refs.pop(0) if outs else None
        out_refs = [refs.pop(0) for _ in outs]
        keep_ref = refs.pop(0) if keep else None
        gathered = refs.pop(0) if pieces else None
        grown_out = refs.pop(0) if outs else None
        raw_rows = refs.pop(0) if raw else None

        def planes_of(place, span):
            _, count, k, extra, flip, share = place
            start = flipped(ids_ref, 0, k, span) + extra
            if share:
                start = start + flipped(ids_ref, 1, flip, share)
            return lambda turn, total: pl.ds(
                pl.multiple_of((turn * total + start) * block, count * block), count * block
            )

        def sign(count):
            lane = lax.broadcasted_iota(jnp.int32, (count, lanes), 1)
            return jnp.where(lane < half, 1.0, -1.0)

        for ref, places_ in zip(ins, places):
            for place in places_:
                count = place[1]
                at = planes_of(place, span[0])
                for turn in range(rows // block):
                    row = turn * block + (first_row if ref.shape[1] > rows else 0)
                    gathered[at(turn, in_count), :] = ref[
                        place[0] : place[0] + count, row : row + block
                    ].reshape(count * block, lanes)

        def main_of(part, turn, line):
            if not raw:
                return main_ref[part, first_row + turn * block + line]
            value = raw_rows[pl.ds(part * depth * block + line, depth, stride=block), :]
            return pack_transfer(value, part, ids_ref[0] >= raw // 2)

        def some(turn, carry):
            if raw:
                row = pl.multiple_of(first_row + turn * block, block)
                raw_rows[...] = main_ref[:, :, pl.ds(row, block), :].reshape(2 * depth * block, lanes)
            for pair in range(block // 2):
                one_pair(turn, (2 * pair, 2 * pair + 1))
            return carry

        def one_pair(turn, lines):
            ks = [turn * block + line for line in lines]
            results = []
            if pieces:
                both = jnp.concatenate(
                    [
                        gathered[pl.ds(turn * in_count * block + line, in_count, stride=block), :]
                        for line in lines
                    ],
                    axis=1,
                )
                grown = dot(forward_ref[...], three(both))
                for index, k in enumerate(ks):
                    lanes_of = slice(index * lanes, (index + 1) * lanes)
                    cos_part, sin_part = grown[:depth, lanes_of], grown[depth:, lanes_of]
                    sin_roll = pltpu.roll(sin_part, half, 1)
                    spectrum = cos_part + sign(depth) * sin_roll
                    result = (
                        spectrum * main_of(0, turn, lines[index])
                        + pltpu.roll(spectrum, half, 1) * (main_of(1, turn, lines[index]) * side)
                    )
                    if lines[index] == 0 and first_row == 0:
                        change = sign(depth) * cos_part - sin_roll - spectrum
                        extra = (
                            change * cross_ref[0]
                            + pltpu.roll(change, half, 1) * cross_ref[1] * side
                        )
                        result = result + jnp.where(turn == 0, extra, 0.0)
                    if added is not None:
                        result = result + added_ref[first_row + k]
                    results.append(result)
            else:
                results = [added_ref[first_row + k] for k in ks]
            if keep:
                for k, result in zip(ks, results):
                    keep_ref[k] = result
            if not outs:
                return
            grown = dot(inverse_ref[...], three(jnp.concatenate(results, axis=1)))
            for index, k in enumerate(ks):
                lanes_of = slice(index * lanes, (index + 1) * lanes)
                cos_part, sin_part = grown[:out_count, lanes_of], grown[out_count:, lanes_of]
                grown_out[
                    pl.ds(turn * out_count * block + lines[index], out_count, stride=block), :
                ] = cos_part - sign(
                    out_count
                ) * pltpu.roll(sin_part, half, 1)

        lax.fori_loop(0, rows // block, some, 0)
        for ref, places_ in zip(out_refs, outs):
            for place in places_:
                count = place[1]
                at = planes_of(place, span[1])
                for turn in range(rows // block):
                    ref[place[0] : place[0] + count, turn * block : (turn + 1) * block] = grown_out[
                        at(turn, out_count), :
                    ].reshape(count, block, lanes)

    results = pl.pallas_call(
        body,
        out_shape=out_shape,
        in_specs=[SMEM] + [VMEM] * len(operands),
        out_specs=[VMEM] * len(out_shape),
        scratch_shapes=scratch,
        interpret=INTERPRET,
        compiler_params=pltpu.CompilerParams(vmem_limit_bytes=VMEM_LIMIT),
        name="depth_step",
    )(ids, *operands)
    return results[: len(outs)], (results[-1] if keep else None)


def rows_of(ref, k):
    planes, count, lanes = ref.shape
    return ref.reshape(planes * count, lanes).at[pl.ds(k, planes, stride=count), :]


def cross_tables(first, space_count):
    _, depth, lanes = first.shape
    half = lanes // 2
    device = lax.axis_index("space")
    upper = device >= space_count // 2
    special = (device % (space_count // 2)) == 0
    other = lax.ppermute(first, "space", [(0, space_count // 2), (space_count // 2, 0)])
    change = jnp.where(special, 0.5 * (first - other), 0.0)
    column = jnp.where(upper, change[:, :, half], change[:, :, 0])[:, :, None]
    lane = lax.broadcasted_iota(jnp.int32, (depth, lanes), 1)
    return jnp.stack(
        [
            jnp.where(lane % half == 0, column[0], 0.0),
            jnp.where(lane == 0, -column[1], jnp.where(lane == half, column[1], 0.0)),
        ]
    )


def pack_transfer(value, part, upper):
    lanes = value.shape[1]
    half = lanes // 2
    lane = lax.broadcasted_iota(jnp.int32, value.shape, 1)
    rolled = pltpu.roll(value, half, 1)
    low = lane < half
    first_lanes = jnp.where(upper, lane, 1) % half == 0
    packed = jnp.where(low ^ first_lanes, value, rolled)
    return packed if part == 0 else jnp.where(low, -packed, packed)


def transfer_table(psf, after, ids, space_count):
    _, depth, rows, lanes = psf.shape
    block = BLOCK_ROWS

    def body(ids_ref, psf_ref, _, main_ref):
        upper = ids_ref[0] >= space_count // 2
        for k in range(block):
            for part in range(2):
                main_ref[part, k] = pack_transfer(rows_of(psf_ref.at[part], k)[...], part, upper)

    return pl.pallas_call(
        body,
        grid_spec=pltpu.PrefetchScalarGridSpec(
            num_scalar_prefetch=1,
            grid=(rows // block,),
            in_specs=[
                pl.BlockSpec((2, depth, block, lanes), lambda i, *_: (0, 0, i, 0)),
                pl.BlockSpec(memory_space=pl.ANY),
            ],
            out_specs=pl.BlockSpec((2, block, depth, lanes), lambda i, *_: (0, i, 0, 0)),
        ),
        out_shape=jax.ShapeDtypeStruct((2, rows, depth, lanes), jnp.float32),
        interpret=INTERPRET,
        compiler_params=pltpu.CompilerParams(vmem_limit_bytes=VMEM_LIMIT),
        name="transfer_table",
    )(ids, psf, after)


def send(array, axis, count, flip):
    if flip == 0:
        return array
    return lax.ppermute(array, axis, [(i, i ^ flip) for i in range(count)])


def add_moved(parts, moved, size, share):
    sums, first = [], 0
    for part in parts:
        count = part.shape[0] // size
        new = moved[first * size : (first + count) * size]
        first += count
        if share:
            sums += [part[i : i + share] + new[i : i + share] for i in range(0, size, share)]
        else:
            sums.append(part + new)
    return sums


def join_planes(ids, copies, flips, planes):
    share, rows, lanes = copies[0].shape
    count = len(copies)

    def body(ids_ref, *refs):
        ins, out_ref, sems = refs[:count], refs[count], refs[count + 1]
        moves = [
            pltpu.make_async_copy(
                ref, out_ref.at[pl.ds(flipped(ids_ref, 1, flip, share), share)], sems.at[i]
            )
            for i, (ref, flip) in enumerate(zip(ins, flips))
        ]
        for move in moves:
            move.start()
        for move in moves:
            move.wait()

    return pl.pallas_call(
        body,
        out_shape=jax.ShapeDtypeStruct((planes, rows, lanes), jnp.float32),
        in_specs=[SMEM] + [ANY] * count,
        out_specs=ANY,
        scratch_shapes=[pltpu.SemaphoreType.DMA((count,))],
        interpret=INTERPRET,
        compiler_params=pltpu.CompilerParams(vmem_limit_bytes=VMEM_LIMIT),
        name="join_planes",
    )(ids, *copies)


def shards(estimate, observed, valid, psf_spectrum):
    space_count = lax.axis_size("space")
    views = lax.axis_size("view")
    planes, row_total, lanes = estimate.shape
    depth = planes * space_count
    part_rows = row_total // space_count
    view_count = views * observed.shape[0]
    columns_f, columns_i = column_tables(lanes, 1.0 / (depth * row_total * lanes))
    rows_f, rows_i, masks_f, masks_i = row_tables(row_total, lanes)
    tables = {
        "forward": (jnp.asarray(columns_f), jnp.asarray(rows_f), jnp.asarray(masks_f)),
        "inverse": (jnp.asarray(columns_i), jnp.asarray(rows_i), jnp.asarray(masks_i)),
    }
    observed, valid = observed[0], valid[0]
    ids = jnp.stack([lax.axis_index("space"), lax.axis_index("view")]).astype(jnp.int32)

    shared = planes % views == 0 and views & (views - 1) == 0
    blocks = views if shared else 1
    share = planes // blocks
    strides = [1 << bit for bit in range(blocks.bit_length() - 1)]
    flips = [0]
    for stride in reversed(strides):
        flips = flips + [f ^ stride for f in flips]
    ks = list(range(space_count))
    chunk = planes // 2 if planes % 2 == 0 else planes
    starts = list(range(0, planes, chunk))
    whole_rows = [(0, part_rows)]
    sum_groups = [flips[:1]] + [flips[1 << bit : 2 << bit] for bit in range(len(strides))]
    turns = part_rows // BLOCK_ROWS
    small = max(3 * turns // 8, 1) * BLOCK_ROWS
    if turns > 1:
        blur_rows = [(0, small), (small, part_rows - small)]
        back_rows = [(0, turns // 2 * BLOCK_ROWS), (turns // 2 * BLOCK_ROWS, (turns + 1) // 2 * BLOCK_ROWS)]
    else:
        blur_rows = back_rows = whole_rows

    def row_places(ranges):
        return [(k, first, count) for first, count in ranges for k in ks]

    slabs = np.arange(space_count)[:, None] * planes
    full_tables = depth_tables(depth, np.arange(depth))
    chunk_tables = [
        depth_tables(depth, (slabs + start + np.arange(chunk)[None, :]).reshape(-1)) for start in starts
    ]
    chunk_places = [[(0, chunk, k, 0, 0, 0)] for k in ks]
    view_share = share if shared else 0

    cross = cross_tables(psf_spectrum[0, :, :, 0, :], space_count)
    own = lax.dynamic_slice_in_dim(estimate, ids[1] * share, share, 0) if shared else estimate
    spectrum = lateral_forward(own, ids, tables, part_rows, row_places(whole_rows))
    transfer = (psf_spectrum[0], cross)

    def spread(pieces):
        moved = []
        for k in ks:
            moved.append(send(pieces[k], "space", space_count, k))
        return moved

    for iteration in range(ITERS):
        last = iteration == ITERS - 1
        pieces, places = [], []
        arrived = spread(spectrum)
        for k, piece in enumerate(arrived):
            copies = [piece]
            for stride in reversed(strides):
                copies = copies + [send(c, "view", views, stride) for c in copies]
            pieces += copies
            places += [[(0, share, k, 0, flip, view_share)] for flip in flips]
        blurred = [[] for _ in starts]
        for shape in blur_rows:
            outs, _ = depth_step(
                ids, pieces, places, None, transfer, full_tables[0], full_tables[1],
                [[(0, chunk, k, start, 0, 0)] for start in starts for k in ks],
                False, False, (planes, planes), shape, 0 if iteration else space_count,
            )
            for number in range(len(starts)):
                blurred[number] += spread(outs[number * space_count : (number + 1) * space_count])
        if iteration == 0:
            transfer = (transfer_table(psf_spectrum[0], outs[0], ids, space_count), cross)
        ratios = []
        for number, start in enumerate(starts):
            final = number == len(starts) - 1
            ratio = ratio_step(
                blurred[number], row_places(blur_rows), observed, valid, start, ids, tables, part_rows,
                row_places(back_rows if final else whole_rows),
            )
            ratios.append(ratio)
        kept = None
        for number, ratio in enumerate(ratios[:-1]):
            arrived = spread(ratio)
            _, kept = depth_step(
                ids, arrived, chunk_places, kept, transfer, chunk_tables[number][0], full_tables[1],
                [], True, True, (chunk, planes), (0, part_rows),
            )
        arrived = []
        for number in range(len(back_rows)):
            arrived.append(spread(ratios[-1][number * space_count : (number + 1) * space_count]))
        combined = []
        for number, shape in enumerate(back_rows):
            parts, _ = depth_step(
                ids, arrived[number], chunk_places, kept, transfer,
                chunk_tables[-1][0], full_tables[1],
                [
                    [
                        (k * share + index * share * space_count, share, k, 0, flip, view_share)
                        for index, flip in enumerate(group)
                        for k in ks
                    ]
                    for group in sum_groups
                ],
                False, True, (chunk, planes), shape,
            )
            for stride, group in zip(strides, reversed(sum_groups)):
                moved = send(parts[-1], "view", views, stride)
                parts = add_moved(parts[:-1], moved, space_count * share, share if len(parts) == 2 else 0)
            if not strides:
                total = parts[0] if shared else lax.psum(parts[0], "view")
                parts = [total[k * share : (k + 1) * share] for k in ks]
            combined += spread(parts)
        own, spectrum = update_step(
            combined, row_places(back_rows), own, float(view_count), ids, tables, part_rows,
            [] if last else row_places(whole_rows),
        )
    if not shared:
        return own
    copies = [own]
    for stride in reversed(strides):
        copies = copies + [send(c, "view", views, stride) for c in copies]
    return join_planes(ids, copies, flips, planes)


def solution(mesh):
    return jax.shard_map(
        shards,
        mesh=mesh,
        in_specs=(
            P("space", "blocks", None),
            P("view", "space", "blocks", None),
            P("view", "space", "blocks", None),
            P("view", None, None, "space", None),
        ),
        out_specs=P("space", "blocks", None),
        check_vma=False,
    )
```
